128 devices in a mesh: seq: 16 (over z, x), head: 8 (over y, core).
Axes of the slice: x: 4, y: 4, z: 4, core: 2. Of those that a mesh axis runs over, the one named last changes fastest.
Arguments:
- x_inputs: bfloat16 [131072, 1024], P('seq', 'head'), may hold values from -6 to 6
- x_in_proj: bfloat16 [131072, 128], P('seq'), may hold values from -0.5 to 0.5
- x_out_proj: bfloat16 [131072, 128], P('seq'), may hold values from -6 to 6
- x_log_decay: float32 [16, 131072], P('head', 'seq'), may hold values from -0.6 to 0
- x_step: float32 [16, 131072], P('head', 'seq'), may hold values from 0 to 0.5
- z_source: int32 [131072], P('seq'), may hold values from 0 to 131071, as said below
- z_in_proj: bfloat16 [131072, 128], P('seq'), may hold values from -0.5 to 0.5
- z_out_proj: bfloat16 [131072, 128], P('seq'), may hold values from -6 to 6
- z_log_decay: float32 [16, 131072], P('head', 'seq'), may hold values from -0.6 to 0
- z_step: float32 [16, 131072], P('head', 'seq'), may hold values from 0 to 0.5
- gate_branch: bfloat16 [131072, 1024], P('seq', 'head'), may hold values from -8 to 8
- norm_gain: float32 [1024], P('head'), may hold values from 0.1 to 1.9
- out_weight: bfloat16 [1024, 512], P('head'), may hold values from -0.1875 to 0.1875
Outputs:
- layer_out: bfloat16 [131072, 512], P(('seq', 'head'))
The draws below stay inside these ranges and needn't reach their ends.
Inputs may be any that keep to these rules, and one draw needn't show every extreme that they name: z_source is a permutation; every block of 8192 consecutive z-order positions takes exactly 512 tokens from each block of 8192 consecutive x-order tokens.
All inputs are finite; a program needn't handle non-finite values.
Results may differ from the reference program's by a relative error of at most 0.034.
Values may be sent and summed in bfloat16 or wider, within the bound.
No kernel may reach another device: no remote copies, remote signals or barrier semaphores. Data moves between devices by JAX's collectives and lax.ppermute only.
A program may use at most 128 MiB of HBM per device.

```python
import math
import jax
import jax.numpy as jnp
from jax import lax

D = 512
HEADS = 16
HEAD_DIM = 64
STATE = 128
BLOCK = 512
TOK_DEV = 8192
HP = 1024
TOKENS = 131072
PEER_ROWS = 512
N_HEAD = 8


def head_rate(key, salt):
    order = jax.random.permutation(jax.random.fold_in(key, salt), HEADS).astype(jnp.float32)
    offset = jax.random.uniform(jax.random.fold_in(key, salt + 5), (HEADS,))
    low = math.log(1.0 / (8.0 * BLOCK))
    high = math.log(1.0 / 32.0)
    return jnp.exp(low + (high - low) * (order + offset) / HEADS)


def decay_draw(key, salt):
    decay_speed = head_rate(key, salt)[:, None]
    spread = math.log(2.0)
    coarse_estimate = jnp.exp(jax.random.uniform(jax.random.fold_in(key, salt + 1), (HEADS, TOKENS), jnp.float32, -spread, spread))
    patch_locations = jax.random.randint(jax.random.fold_in(key, salt + 2), (HEADS, 2), 0, TOKENS)
    token_place = jnp.arange(TOKENS, dtype=jnp.int32)[None, :]
    sudden_spike = (token_place == patch_locations[:, 0:1]) | (token_place == patch_locations[:, 1:2])
    retained_mask = jax.random.uniform(jax.random.fold_in(key, salt + 3), (HEADS, TOKENS), jnp.float32, 0.6, 0.8)
    return -decay_speed * coarse_estimate + jnp.where(sudden_spike, jnp.log(retained_mask), 0.0)


def step_draw(key, salt):
    decay_speed = head_rate(key, salt)[:, None]
    spread = math.log(2.0)
    coarse_estimate = jnp.exp(jax.random.uniform(jax.random.fold_in(key, salt + 4), (HEADS, TOKENS), jnp.float32, -spread, spread))
    return jnp.sqrt(2.0 * decay_speed) * coarse_estimate


def draw_x_log_decay(key, part):
    return decay_draw(key, 11)


def draw_x_step(key, part):
    return step_draw(key, 11)


def draw_z_log_decay(key, part):
    return decay_draw(key, 31)


def draw_z_step(key, part):
    return step_draw(key, 31)


def draw_z_source(key, part):
    group_sets = TOK_DEV // PEER_ROWS
    keys_dest = jax.random.split(jax.random.fold_in(key, 51), group_sets)
    keys_source = jax.random.split(jax.random.fold_in(key, 52), group_sets)
    sigma = jax.vmap(lambda subkey: jax.random.permutation(subkey, TOK_DEV))(keys_dest)
    tau = jax.vmap(lambda subkey: jax.random.permutation(subkey, TOK_DEV))(keys_source)
    source = sigma % group_sets
    slot = jnp.arange(group_sets, dtype=jnp.int32)[:, None] * PEER_ROWS + sigma // group_sets
    result = source * TOK_DEV + tau[source, slot]
    return result.reshape(TOKENS).astype(jnp.int32)


def draw_gate_branch(key, part):
    channel = jnp.arange(HP, dtype=jnp.float32) / HP
    noise = jnp.clip(jax.random.normal(jax.random.fold_in(key, 71), (TOKENS, HP), jnp.float32), -4.0, 4.0)
    scale = 0.6 * jnp.power(3.0, channel)
    return (noise * scale[None, :]).astype(jnp.bfloat16)


def levels(own_key, shape, cuts, low, top_value):
    factor_of, own = 1.0, jax.random.fold_in(own_key, 6)
    for axis_at, shards_of in cuts:
        steps = jnp.exp(jax.random.uniform(jax.random.fold_in(own, axis_at), (shards_of,), jnp.float32, low / len(cuts), top_value / len(cuts)))
        factor_of = factor_of * jnp.repeat(steps, shape[axis_at] // shards_of).reshape([-1 if axis == axis_at else 1 for axis in range(len(shape))])
    return factor_of


def normal_values(own_key, shape, deviation, most, cuts=(), kind=jnp.bfloat16):
    entries = deviation * jax.random.normal(own_key, shape, jnp.float32)
    if cuts:
        entries = entries * levels(own_key, shape, cuts, -0.22, 0.18)
    return jnp.clip(entries, -most, most).astype(kind)


def setup_inputs(seed: int = 0) -> dict:
    arg_keys = jax.random.split(jax.random.key(seed), 14)
    x_inputs = normal_values(arg_keys[0], (TOKENS, HP), 1.0, 6.0, ((0, 16), (1, 8)))
    x_in_proj = normal_values(arg_keys[1], (TOKENS, STATE), STATE ** -0.5, 0.5, ((0, 16),))
    x_out_proj = normal_values(arg_keys[2], (TOKENS, STATE), 1.0, 6.0, ((0, 16),))
    x_log_decay = draw_x_log_decay(jax.random.fold_in(arg_keys[13], 71), 0)
    x_step = draw_x_step(jax.random.fold_in(arg_keys[13], 71), 0)
    z_source = draw_z_source(jax.random.fold_in(arg_keys[13], 71), 0)
    z_in_proj = normal_values(arg_keys[6], (TOKENS, STATE), STATE ** -0.5, 0.5, ((0, 16),))
    z_out_proj = normal_values(arg_keys[7], (TOKENS, STATE), 1.0, 6.0, ((0, 16),))
    z_log_decay = draw_z_log_decay(jax.random.fold_in(arg_keys[13], 71), 0)
    z_step = draw_z_step(jax.random.fold_in(arg_keys[13], 71), 0)
    gate_branch = draw_gate_branch(jax.random.fold_in(arg_keys[13], 71), 0)
    norm_gain = jnp.clip(1.0 + 0.18 * jax.random.normal(arg_keys[11], (HP,), jnp.float32), 0.1, 1.9)
    out_weight = normal_values(arg_keys[12], (HP, D), HP ** -0.5, 0.1875, ((0, 8),))
    return {"x_inputs": x_inputs, "x_in_proj": x_in_proj, "x_out_proj": x_out_proj, "x_log_decay": x_log_decay, "x_step": x_step, "z_source": z_source, "z_in_proj": z_in_proj, "z_out_proj": z_out_proj, "z_log_decay": z_log_decay, "z_step": z_step, "gate_branch": gate_branch, "norm_gain": norm_gain, "out_weight": out_weight}


def round_half(value):
    return lax.optimization_barrier(value.astype(jnp.bfloat16)).astype(jnp.float32)

def ssd_scan(inputs, b_mat, c_mat, log_decay, step):
    count = inputs.shape[0]
    blocks = count // BLOCK
    u_blocks = inputs.reshape(blocks, BLOCK, HEADS, HEAD_DIM)
    b_blocks = b_mat.reshape(blocks, BLOCK, STATE)
    c_blocks = c_mat.reshape(blocks, BLOCK, STATE)
    g_blocks = log_decay.reshape(HEADS, blocks, BLOCK).transpose(1, 0, 2)
    d_blocks = step.reshape(HEADS, blocks, BLOCK).transpose(1, 0, 2)
    rows = lax.broadcasted_iota(jnp.int32, (BLOCK, BLOCK), 0)
    cols = lax.broadcasted_iota(jnp.int32, (BLOCK, BLOCK), 1)
    lower = rows >= cols

    def one_block(carry, pieces):
        u_blk, b_blk, c_blk, g_blk, d_blk = pieces
        cum = jnp.cumsum(g_blk, axis=1)
        tot = cum[:, -1]
        scores = jnp.dot(c_blk, b_blk.T, preferred_element_type=jnp.float32)
        diff = jnp.where(lower[None], cum[:, :, None] - cum[:, None, :], -jnp.inf)
        weights = round_half(scores[None] * jnp.exp(diff) * d_blk[:, None, :])
        u_float = u_blk.astype(jnp.float32)
        intra = jnp.einsum('hts,shp->thp', weights, u_float)
        scale = (jnp.exp(tot[:, None] - cum) * d_blk).T
        contrib = round_half(u_float * scale[:, :, None])
        state_add = jnp.einsum('shp,sn->hpn', contrib, b_blk.astype(jnp.float32))
        inter = jnp.einsum('tn,hpn->thp', c_blk.astype(jnp.float32), round_half(carry))
        inter = inter * jnp.exp(cum).T[:, :, None]
        result = (intra + inter).astype(jnp.bfloat16).reshape(BLOCK, HEADS * HEAD_DIM)
        carry = jnp.exp(tot)[:, None, None] * carry + state_add
        return (carry, result)
    start = jnp.zeros((HEADS, HEAD_DIM, STATE), jnp.float32)
    _, outputs = lax.scan(one_block, start, (u_blocks, b_blocks, c_blocks, g_blocks, d_blocks))
    return outputs.reshape(count, HEADS * HEAD_DIM)

def reference(x_inputs, x_in_proj, x_out_proj, x_log_decay, x_step, z_source, z_in_proj, z_out_proj, z_log_decay, z_step, gate_branch, norm_gain, out_weight):
    y_x = ssd_scan(x_inputs, x_in_proj, x_out_proj, x_log_decay, x_step)
    u_z = jnp.take(y_x, z_source.astype(jnp.int32), axis=0)
    y_z = ssd_scan(u_z, z_in_proj, z_out_proj, z_log_decay, z_step)
    gated = y_z.astype(jnp.float32) * jax.nn.silu(gate_branch.astype(jnp.float32))
    mean_square = lax.optimization_barrier(jnp.mean(gated * gated, axis=1, keepdims=True))
    normed = (gated * lax.rsqrt(mean_square + 1e-05) * norm_gain).astype(jnp.bfloat16)
    group = HP // N_HEAD
    total = jnp.zeros((normed.shape[0], D), jnp.float32)
    for index in range(N_HEAD):
        partial_sum = jnp.dot(normed[:, index * group:(index + 1) * group], out_weight[index * group:(index + 1) * group], preferred_element_type=jnp.float32)
        total = total + round_half(partial_sum)
    return total.astype(jnp.bfloat16)
```

```python
import functools

import jax
import jax.numpy as jnp
from jax import lax
from jax.experimental import pallas as pl
from jax.experimental.pallas import tpu as pltpu
from jax.sharding import PartitionSpec as P

TOK = 8192
LANES = 128
CHUNK = 128
STEP = 1024
STEPS = TOK // STEP
PIECE = 512
GROUPS = 16
TAIL = 144
MSG = 160
F32 = jnp.float32
BF16 = jnp.bfloat16


def mm(a, b):
    return jnp.dot(a, b, preferred_element_type=F32)


def per_channel(rows, at):
    part = rows[:, at * CHUNK : (at + 1) * CHUNK]
    high = part.astype(BF16).astype(F32)
    low = part - high
    both = jnp.concatenate([high, low], axis=1)
    wide = jnp.concatenate(
        [jnp.broadcast_to(both[0:1], (64, 2 * CHUNK)), jnp.broadcast_to(both[1:2], (64, 2 * CHUNK))], axis=0
    )
    return wide.astype(BF16)


def nt(a, b):
    return lax.dot_general(a, b, (((1,), (1,)), ((), ())), preferred_element_type=F32)


def masks():
    row = lax.broadcasted_iota(jnp.int32, (CHUNK, CHUNK), 0)
    col = lax.broadcasted_iota(jnp.int32, (CHUNK, CHUNK), 1)
    lower = row >= col
    tri = jnp.where(lower, 1.0, 0.0).astype(BF16)
    eye = jnp.where(row == col, 1.0, 0.0).astype(BF16)
    return lower, jnp.concatenate([tri, tri], axis=1), jnp.concatenate([eye, eye], axis=1)


def scan_states(g_ref, d_ref, b_ref, read_u, u2_ref, msg_ref, state, total, first, last):
    _, tri, eye = masks()

    @pl.when(first)
    def _():
        state[...] = jnp.zeros_like(state)
        total[...] = jnp.zeros_like(total)

    carry = state[...]
    sums = total[0:1, :]
    for at in range(STEP // CHUNK):
        rows = slice(at * CHUNK, (at + 1) * CHUNK)
        cum = nt(tri, per_channel(g_ref, at))
        step = nt(eye, per_channel(d_ref, at))
        mid = cum[CHUNK // 2 - 1 : CHUNK // 2]
        tot = cum[CHUNK - 1 : CHUNK]
        u2 = (read_u(at) * (jnp.exp(mid - cum) * step)).astype(BF16)
        u2_ref[rows, :] = u2
        carry = jnp.exp(tot) * carry + jnp.exp(tot - mid) * mm(b_ref[rows, :].T, u2)
        sums = sums + tot
    state[...] = carry
    total[0:1, :] = sums

    @pl.when(last)
    def _():
        high = sums.astype(BF16).astype(F32)
        mid = (sums - high).astype(BF16).astype(F32)
        low = sums - high - mid
        pad = jnp.zeros((TAIL - CHUNK - 3, LANES), F32)
        msg_ref[...] = jnp.concatenate([carry, high, mid, low, pad], axis=0).astype(BF16)


def states_x_kernel(g_ref, d_ref, b_ref, u_ref, u2_ref, msg_ref, state, total):
    step = pl.program_id(0)

    def read_u(at):
        return u_ref[at * CHUNK : (at + 1) * CHUNK, :].astype(F32)

    scan_states(g_ref, d_ref, b_ref, read_u, u2_ref, msg_ref, state, total, step == 0, step == STEPS - 1)


def states_z_kernel(place, g_ref, d_ref, b_ref, got_ref, u2_ref, msg_ref, state, total, wide, ordered):
    step = pl.program_id(0)

    @pl.when(step < STEPS)
    def _():
        wide[...] = got_ref[...].astype(F32)

        def put(i, _):
            for k in range(16):
                row = i * 16 + k
                ordered[pl.ds(place[step * STEP + row], 1), :] = wide[pl.ds(row, 1), :]
            return 0

        lax.fori_loop(0, STEP // 16, put, 0)

    @pl.when(step >= STEPS)
    def _():
        base = (step - STEPS) * STEP

        def read_u(at):
            return ordered[pl.ds(pl.multiple_of(base + at * CHUNK, CHUNK), CHUNK), :]

        scan_states(
            g_ref, d_ref, b_ref, read_u, u2_ref, msg_ref, state, total, step == STEPS, step == 2 * STEPS - 1
        )


def start_state(got_ref, state):
    me = lax.axis_index("seq")
    state[...] = jnp.zeros_like(state)
    for k in range(GROUPS - 1):

        @pl.when(k < me)
        def _():
            tail = got_ref[k, CHUNK:TAIL, :].astype(F32)
            decay = jnp.exp(tail[0:1] + tail[1:2] + tail[2:3])
            state[...] = decay * state[...] + got_ref[k, 0:CHUNK, :].astype(F32)


def scan_outputs(g_ref, b_ref, c_ref, u2_ref, state, write):
    lower, tri, _ = masks()
    carry = state[...]
    for at in range(STEP // CHUNK):
        rows = slice(at * CHUNK, (at + 1) * CHUNK)
        cum = nt(tri, per_channel(g_ref, at))
        mid = cum[CHUNK // 2 - 1 : CHUNK // 2]
        tot = cum[CHUNK - 1 : CHUNK]
        b_t = b_ref[rows, :].T
        c_blk = c_ref[rows, :]
        u2 = u2_ref[rows, :]
        scores = jnp.where(lower, mm(c_blk, b_t), 0.0).astype(BF16)
        held = (carry * jnp.exp(mid)).astype(BF16)
        left = jnp.concatenate([scores, c_blk], axis=1)
        right = jnp.concatenate([u2, held], axis=0)
        write(at, jnp.exp(cum - mid) * mm(left, right))
        carry = jnp.exp(tot) * carry + jnp.exp(tot - mid) * mm(b_t, u2)
    state[...] = carry


def outputs_x_kernel(pick, g_ref, b_ref, c_ref, u2_ref, got_ref, out_ref, state, y_all, rows_ref):
    step = pl.program_id(0)

    @pl.when(step == 0)
    def _():
        start_state(got_ref, state)

    @pl.when(step < STEPS)
    def _():
        def write(at, value):
            y_all[pl.ds(pl.multiple_of(step * STEP + at * CHUNK, CHUNK), CHUNK), :] = value

        scan_outputs(g_ref, b_ref, c_ref, u2_ref, state, write)

    @pl.when(step >= STEPS)
    def _():
        base = (step - STEPS) * STEP

        def take(i, _):
            for k in range(16):
                row = i * 16 + k
                rows_ref[pl.ds(row, 1), :] = y_all[pl.ds(pick[base + row], 1), :]
            return 0

        lax.fori_loop(0, STEP // 16, take, 0)
        out_ref[...] = rows_ref[...].astype(BF16)


def outputs_z_kernel(g_ref, b_ref, c_ref, u2_ref, gate_ref, got_ref, out_ref, state):
    @pl.when(pl.program_id(0) == 0)
    def _():
        start_state(got_ref, state)

    def write(at, value):
        rows = slice(at * CHUNK, (at + 1) * CHUNK)
        gate = gate_ref[rows, :].astype(F32)
        silu = gate / (1.0 + jnp.exp(-gate))
        out_ref[rows, :] = (value.astype(BF16).astype(F32) * silu).astype(BF16)

    scan_outputs(g_ref, b_ref, c_ref, u2_ref, state, write)


def final_kernel(x_ref, w_ref, out_ref):
    parts = [x_ref[k].astype(F32) for k in range(8)]
    squares = sum(part * part for part in parts)
    mean = jnp.sum(squares, axis=1, keepdims=True) * (1.0 / 1024.0)
    scale = lax.rsqrt(mean + 1e-05)
    total = None
    for k in range(8):
        pieces = w_ref[k, LANES:TAIL, 0:LANES].astype(F32)
        gain = pieces[0:1] + pieces[1:2] + pieces[2:3]
        term = mm((parts[k] * scale * gain).astype(BF16), w_ref[k, 0:LANES, :])
        total = term if total is None else total + term
    out_ref[...] = total.astype(BF16)


def spec(shape, index):
    return pl.BlockSpec(shape, index)


def params():
    return pltpu.CompilerParams(dimension_semantics=("arbitrary",), vmem_limit_bytes=48 * 1024 * 1024)


def cost(flops, bytes_accessed):
    return pl.CostEstimate(flops=flops, bytes_accessed=bytes_accessed, transcendentals=0)


ROW = (STEP, LANES)
PAIR = (2, STEP)
STATE_SCRATCH = [pltpu.VMEM((CHUNK, LANES), F32)]


def states_x(g, d, b, u):
    return pl.pallas_call(
        states_x_kernel,
        name="states_x",
        grid=(STEPS,),
        in_specs=[
            spec(PAIR, lambda i: (0, i)),
            spec(PAIR, lambda i: (0, i)),
            spec(ROW, lambda i: (i, 0)),
            spec(ROW, lambda i: (i, 0)),
        ],
        out_specs=[spec(ROW, lambda i: (i, 0)), spec((TAIL, LANES), lambda i: (0, 0))],
        out_shape=[jax.ShapeDtypeStruct((TOK, LANES), BF16), jax.ShapeDtypeStruct((TAIL, LANES), BF16)],
        scratch_shapes=STATE_SCRATCH + [pltpu.VMEM((8, LANES), F32)],
        compiler_params=params(),
        cost_estimate=cost(2 * TOK * 128 * 640, 6 << 20),
    )(g, d, b, u)


def states_z(place, g, d, b, got):
    late = lambda i, _: (jnp.maximum(i - STEPS, 0), 0)
    late_pair = lambda i, _: (0, jnp.maximum(i - STEPS, 0))
    return pl.pallas_call(
        states_z_kernel,
        name="states_z",
        grid_spec=pltpu.PrefetchScalarGridSpec(
            num_scalar_prefetch=1,
            grid=(2 * STEPS,),
            in_specs=[
                spec(PAIR, late_pair),
                spec(PAIR, late_pair),
                spec(ROW, late),
                spec(ROW, lambda i, _: (jnp.minimum(i, STEPS - 1), 0)),
            ],
            out_specs=[spec(ROW, late), spec((TAIL, LANES), lambda i, _: (0, 0))],
            scratch_shapes=STATE_SCRATCH
            + [pltpu.VMEM((8, LANES), F32), pltpu.VMEM(ROW, F32), pltpu.VMEM((TOK, LANES), F32)],
        ),
        out_shape=[jax.ShapeDtypeStruct((TOK, LANES), BF16), jax.ShapeDtypeStruct((TAIL, LANES), BF16)],
        compiler_params=params(),
        cost_estimate=cost(2 * TOK * 128 * 640, 6 << 20),
    )(place, g, d, b, got)


def outputs_x(pick, g, b, c, u2, got):
    early = lambda i, _: (jnp.minimum(i, STEPS - 1), 0)
    return pl.pallas_call(
        outputs_x_kernel,
        name="outputs_x",
        grid_spec=pltpu.PrefetchScalarGridSpec(
            num_scalar_prefetch=1,
            grid=(2 * STEPS,),
            in_specs=[
                spec(PAIR, lambda i, _: (0, jnp.minimum(i, STEPS - 1))),
                spec(ROW, early),
                spec(ROW, early),
                spec(ROW, early),
                spec((GROUPS, MSG, LANES), lambda i, _: (0, 0, 0)),
            ],
            out_specs=spec(ROW, lambda i, _: (jnp.maximum(i - STEPS, 0), 0)),
            scratch_shapes=STATE_SCRATCH + [pltpu.VMEM((TOK, LANES), F32), pltpu.VMEM(ROW, F32)],
        ),
        out_shape=jax.ShapeDtypeStruct((TOK, LANES), BF16),
        compiler_params=params(),
        cost_estimate=cost(2 * TOK * 128 * 896, 8 << 20),
    )(pick, g, b, c, u2, got)


def outputs_z(g, b, c, u2, gate, got):
    return pl.pallas_call(
        outputs_z_kernel,
        name="outputs_z",
        grid=(STEPS,),
        in_specs=[
            spec(PAIR, lambda i: (0, i)),
            spec(ROW, lambda i: (i, 0)),
            spec(ROW, lambda i: (i, 0)),
            spec(ROW, lambda i: (i, 0)),
            spec(ROW, lambda i: (i, 0)),
            spec((GROUPS, TAIL, LANES), lambda i: (0, 0, 0)),
        ],
        out_specs=spec(ROW, lambda i: (i, 0)),
        out_shape=jax.ShapeDtypeStruct((TOK, LANES), BF16),
        scratch_shapes=STATE_SCRATCH,
        compiler_params=params(),
        cost_estimate=cost(2 * TOK * 128 * 896, 10 << 20),
    )(g, b, c, u2, gate, got)


def final(x, w):
    rows = 256
    return pl.pallas_call(
        final_kernel,
        name="final",
        grid=(1024 // rows,),
        in_specs=[
            spec((8, rows, LANES), lambda i: (0, i, 0)),
            spec((8, TAIL, 512), lambda i: (0, 0, 0)),
        ],
        out_specs=spec((rows, 512), lambda i: (i, 0)),
        out_shape=jax.ShapeDtypeStruct((1024, 512), BF16),
        compiler_params=params(),
        cost_estimate=cost(2 * 1024 * 1024 * 512, 5 << 20),
    )(x, w)


def three_pieces(value):
    high = lax.reduce_precision(value, 8, 7)
    mid = lax.reduce_precision(value - high, 8, 7)
    return high, mid, value - high - mid


def body(
    x_inputs,
    x_in_proj,
    x_out_proj,
    x_log_decay,
    x_step,
    z_source,
    z_in_proj,
    z_out_proj,
    z_log_decay,
    z_step,
    gate_branch,
    norm_gain,
    out_weight,
):
    order = jnp.sort(z_source * TOK + lax.iota(jnp.int32, TOK))
    place = order & (TOK - 1)
    source = (order >> 13) & (TOK - 1)
    lists = jnp.concatenate(
        [(source >> 6).reshape(GROUPS, 4, LANES), (source & 63).reshape(GROUPS, 4, LANES)], axis=1
    ).astype(BF16)

    gain = jnp.pad(jnp.stack(three_pieces(norm_gain)), ((0, TAIL - LANES - 3), (0, 512 - LANES))).astype(BF16)
    weights = lax.all_gather(jnp.concatenate([out_weight, gain], axis=0), "head", axis=0, tiled=False)

    u2_x, tail_x = states_x(x_log_decay, x_step, x_in_proj, x_inputs)
    message = jnp.concatenate(
        [
            jnp.broadcast_to(tail_x[None], (GROUPS, TAIL, LANES)),
            lists,
            jnp.zeros((GROUPS, MSG - TAIL - 8, LANES), BF16),
        ],
        axis=1,
    )
    got_x = lax.all_to_all(message, "seq", 0, 0)
    wanted = got_x[:, TAIL : TAIL + 8].astype(jnp.int32)
    pick = (wanted[:, 0:4] * 64 + wanted[:, 4:8]).reshape(TOK)
    sent = outputs_x(pick, x_log_decay, x_in_proj, x_out_proj, u2_x, got_x)
    received = lax.all_to_all(sent.reshape(GROUPS, PIECE, LANES), "seq", 0, 0).reshape(TOK, LANES)
    u2_z, tail_z = states_z(place, z_log_decay, z_step, z_in_proj, received)
    got_z = lax.all_to_all(jnp.broadcast_to(tail_z[None], (GROUPS, TAIL, LANES)), "seq", 0, 0)
    gated = outputs_z(z_log_decay, z_in_proj, z_out_proj, u2_z, gate_branch, got_z)
    whole = lax.all_to_all(gated.reshape(8, 1024, LANES), "head", 0, 0)
    return final(whole, weights)


def solution(mesh):
    placed = (
        P("seq", "head"),
        P("seq", None),
        P("seq", None),
        P("head", "seq"),
        P("head", "seq"),
        P("seq"),
        P("seq", None),
        P("seq", None),
        P("head", "seq"),
        P("head", "seq"),
        P("seq", "head"),
        P("head"),
        P("head", None),
    )
    return jax.shard_map(
        body, mesh=mesh, in_specs=placed, out_specs=P(("seq", "head"), None), check_vma=False
    )
```

```python
import functools

import jax
import jax.numpy as jnp
from jax import lax
from jax.experimental import pallas as pl
from jax.experimental.pallas import tpu as pltpu
from jax.sharding import PartitionSpec as P

TOK = 8192
LANES = 128
CHUNK = 128
STEP = 1024
PER = STEP // CHUNK
STEPS = TOK // STEP
PIECE = 512
GROUPS = 16
TAIL = 136
MSG = 144
UNROLL = 32
F32 = jnp.float32
BF16 = jnp.bfloat16


def mm(a, b):
    return jnp.dot(a, b, preferred_element_type=F32)


def nt(a, b):
    return lax.dot_general(a, b, (((1,), (1,)), ((), ())), preferred_element_type=F32)


def tn(a, b):
    return lax.dot_general(a, b, (((0,), (0,)), ((), ())), preferred_element_type=F32)


def iotas():
    shape = (CHUNK, CHUNK)
    return lax.broadcasted_iota(jnp.int32, shape, 0), lax.broadcasted_iota(jnp.int32, shape, 1)


def ones(condition):
    return jnp.where(condition, 1.0, 0.0).astype(BF16)


def pieces(value, axis):
    high = value.astype(BF16)
    rest = value - high.astype(F32)
    mid = rest.astype(BF16)
    low = (rest - mid.astype(F32)).astype(BF16)
    return jnp.concatenate([high, mid, low], axis=axis)


def thrice(mask, axis):
    return jnp.concatenate([mask, mask, mask], axis=axis)


def wide(column):
    return jnp.broadcast_to(column, (CHUNK, LANES))


def by_head(first, second):
    return jnp.where(lax.broadcasted_iota(jnp.int32, (1, LANES), 1) < 64, first, second)


def row_pair(slab, at):
    return by_head(slab[2 * at : 2 * at + 1], slab[2 * at + 1 : 2 * at + 2])


def spread_mask():
    row = lax.broadcasted_iota(jnp.int32, (48, STEP), 0) & 15
    col = lax.broadcasted_iota(jnp.int32, (48, STEP), 1)
    return ones(row == 2 * (col >> 7) + ((col >> 6) & 1))


def spread(slab, mask):
    return tn(pieces(slab, 0), mask)


def slab_at(step):
    return pl.ds(pl.multiple_of(16 * step, 16), 16)


def end_weights(g, d):
    row, col = iotas()
    inner = mm(pieces(g, 1), thrice(ones(row > col), 0))
    total = wide(inner[:, 0:1] + g[:, 0:1])
    later = mm(thrice(ones((col > row) & ((col & 1) == (row & 1))), 1), pieces(total, 0))
    whole = later[0:2] + total[0:2]
    return jnp.exp(inner + later) * d, by_head(whole[0:1], whole[1:2])


def scan_factors(g, d):
    row, col = iotas()
    cum = mm(pieces(g, 1), thrice(ones(row <= col), 0))
    mid = wide(cum[:, CHUNK // 2 - 1 : CHUNK // 2])
    total = wide(cum[:, CHUNK - 1 : CHUNK])
    before = mm(thrice(ones((col < row) & ((col & 1) == (row & 1))), 1), pieces(total, 0))
    return (
        jnp.exp(mid - cum) * d,
        jnp.exp(cum - mid),
        jnp.exp(mid),
        jnp.exp(total),
        jnp.exp(total - mid),
        jnp.exp(mid + before),
    )


def write_tail(msg_ref, state, total):
    high = total.astype(BF16).astype(F32)
    mid = (total - high).astype(BF16).astype(F32)
    low = total - high - mid
    pad = jnp.zeros((TAIL - CHUNK - 3, LANES), F32)
    msg_ref[...] = jnp.concatenate([state, high, mid, low, pad], axis=0).astype(BF16)


def chunk_rows(at):
    return slice(at * CHUNK, (at + 1) * CHUNK)


def states_x_kernel(g_ref, d_ref, b_ref, u_ref, msg_ref, weights, mask, state, total):
    step = pl.program_id(0)

    @pl.when(step == 0)
    def _():
        weights[...], total[0:1, :] = end_weights(g_ref[...], d_ref[...])
        mask[...] = spread_mask()
        state[...] = jnp.zeros_like(state)

    scale = spread(weights[slab_at(step), :], mask[...])
    parts = [
        (u_ref[chunk_rows(at), :].astype(F32) * scale[:, chunk_rows(at)]).astype(BF16) for at in range(PER)
    ]
    state[...] += tn(b_ref[...], jnp.concatenate(parts, axis=0))

    @pl.when(step == STEPS - 1)
    def _():
        write_tail(msg_ref, state[...], total[0:1, :])


def local_scan(u2s, scores, b_ts, cs, slabs, r_slab, mask, state, y_ref):
    into, end, add = slabs
    carry = state[...]
    sums = [mm(b_ts[at], u2s[at]) for at in range(PER)]
    helds = []
    for at in range(PER):
        helds.append((carry * row_pair(into, at)).astype(BF16))
        carry = row_pair(end, at) * carry + row_pair(add, at) * sums[at]
    state[...] = carry
    back = spread(r_slab, mask)
    for at in range(PER):
        left = jnp.concatenate([scores[at], cs[at]], axis=1)
        right = jnp.concatenate([u2s[at], helds[at]], axis=0)
        y_ref[chunk_rows(at), :] = back[:, chunk_rows(at)] * mm(left, right)


def local_x_kernel(g_ref, d_ref, b_ref, c_ref, u_ref, y_ref, r_ref, e_ref, a_all, ends, mask, state):
    step = pl.program_id(0)

    @pl.when(step == 0)
    def _():
        a_all[...], r_ref[...], ends[0], ends[1], ends[2], e_ref[...] = scan_factors(g_ref[...], d_ref[...])
        mask[...] = spread_mask()
        state[...] = jnp.zeros_like(state)

    row, col = iotas()
    lower = row >= col
    here = slab_at(step)
    scale = spread(a_all[here, :], mask[...])
    u2s = [(u_ref[chunk_rows(at), :].astype(F32) * scale[:, chunk_rows(at)]).astype(BF16) for at in range(PER)]
    b_ts = [b_ref[chunk_rows(at), :].T for at in range(PER)]
    cs = [c_ref[chunk_rows(at), :] for at in range(PER)]
    scores = [jnp.where(lower, mm(cs[at], b_ts[at]), 0.0).astype(BF16) for at in range(PER)]
    slabs = (ends[0, here, :], ends[1, here, :], ends[2, here, :])
    local_scan(u2s, scores, b_ts, cs, slabs, r_ref[here, :], mask[...], state, y_ref)


def start_state(got_ref, state):
    me = lax.axis_index("seq")
    state[...] = jnp.zeros_like(state)
    for k in range(GROUPS - 1):

        @pl.when(k < me)
        def _():
            tail = got_ref[k, CHUNK:TAIL, :].astype(F32)
            decay = jnp.exp(tail[0:1] + tail[1:2] + tail[2:3])
            state[...] = decay * state[...] + got_ref[k, 0:CHUNK, :].astype(F32)


def add_start(y_ref, c_ref, r_slab, e_slab, mask, state, write):
    back = spread(r_slab, mask)
    start = state[...]
    for at in range(PER):
        held = (start * row_pair(e_slab, at)).astype(BF16)
        write(at, y_ref[chunk_rows(at), :] + back[:, chunk_rows(at)] * mm(c_ref[chunk_rows(at), :], held))


def invert_lists(got_ref, slots):
    high = lax.broadcasted_iota(jnp.int32, (64, LANES), 0).astype(F32)
    low = lax.broadcasted_iota(jnp.int32, (LANES, LANES), 0).astype(F32)
    lane = lax.broadcasted_iota(jnp.int32, (64, LANES), 1).astype(F32)
    total = jnp.zeros((LANES, LANES), F32)
    for k in range(GROUPS):
        lists = got_ref[k, TAIL:MSG, :].astype(F32)
        lefts, rights = [], []
        for q in range(4):
            hit = high == lists[q : q + 1]
            lefts.append(
                jnp.concatenate([jnp.where(hit, float(4 * k + q), 0.0), jnp.where(hit, lane, 0.0)], axis=0).astype(BF16)
            )
            rights.append(ones(low == lists[4 + q : 5 + q]))
        total = total + nt(jnp.concatenate(lefts, axis=1), jnp.concatenate(rights, axis=1))
    slots[...] = (total[0:64] * 128.0 + total[64:128]).astype(jnp.int32)


def send_x_kernel(
    y_ref, c_ref, r_ref, e_ref, got_ref, out_ref, state, mask, rows, ordered, slots, table, sem
):
    step = pl.program_id(0)

    @pl.when(step == 0)
    def _():
        invert_lists(got_ref, slots)
        copy = pltpu.make_async_copy(slots, table, sem)
        copy.start()
        start_state(got_ref, state)
        mask[...] = spread_mask()
        copy.wait()

    @pl.when(step < STEPS)
    def _():
        here = slab_at(step)

        def write(at, value):
            rows[chunk_rows(at), :] = value

        add_start(y_ref, c_ref, r_ref[here, :], e_ref[here, :], mask[...], state, write)

        def put(i, _):
            line = step * PER + i // 4
            base = (i % 4) * UNROLL
            for k in range(UNROLL):
                ordered[pl.ds(table[line, base + k], 1), :] = rows[pl.ds(i * UNROLL + k, 1), :]
            return 0

        lax.fori_loop(0, STEP // UNROLL, put, 0)

    @pl.when(step >= STEPS)
    def _():
        base = pl.multiple_of((step - STEPS) * STEP, STEP)
        out_ref[...] = ordered[pl.ds(base, STEP), :].astype(BF16)


def before_z_kernel(
    g_ref, d_ref, b_ref, c_ref, s_ref, b_t_ref, w_ref, t_ref, a_ref, r_ref, e_ref, ends_ref
):
    @pl.when(pl.program_id(0) == 0)
    def _():
        w_ref[...], total = end_weights(g_ref[...], d_ref[...])
        t_ref[...] = jnp.broadcast_to(total, (8, LANES))
        a_ref[...], r_ref[...], ends_ref[0], ends_ref[1], ends_ref[2], e_ref[...] = scan_factors(
            g_ref[...], d_ref[...]
        )

    row, col = iotas()
    lower = row >= col
    for at in range(PER):
        b_t = b_ref[chunk_rows(at), :].T
        b_t_ref[:, chunk_rows(at)] = b_t
        s_ref[chunk_rows(at), :] = jnp.where(lower, mm(c_ref[chunk_rows(at), :], b_t), 0.0).astype(BF16)


def states_z_kernel(place, w_ref, t_ref, a_ref, b_t_ref, got_ref, u2_ref, msg_ref, mask, state, rows, ordered):
    step = pl.program_id(0)

    @pl.when(step == 0)
    def _():
        mask[...] = spread_mask()
        state[...] = jnp.zeros_like(state)

    @pl.when(step < STEPS)
    def _():
        rows[...] = got_ref[...].astype(F32)

        def put(i, _):
            base = step * STEP + i * UNROLL
            for k in range(UNROLL):
                ordered[pl.ds(place[base + k], 1), :] = rows[pl.ds(i * UNROLL + k, 1), :]
            return 0

        lax.fori_loop(0, STEP // UNROLL, put, 0)

    @pl.when(step >= STEPS)
    def _():
        base = (step - STEPS) * STEP
        here = slab_at(step - STEPS)
        weight = spread(w_ref[here, :], mask[...])
        scale = spread(a_ref[here, :], mask[...])
        parts = []
        for at in range(PER):
            u = ordered[pl.ds(pl.multiple_of(base + at * CHUNK, CHUNK), CHUNK), :]
            u2_ref[chunk_rows(at), :] = (u * scale[:, chunk_rows(at)]).astype(BF16)
            parts.append((u * weight[:, chunk_rows(at)]).astype(BF16))
        state[...] += mm(b_t_ref[...], jnp.concatenate(parts, axis=0))

    @pl.when(step == 2 * STEPS - 1)
    def _():
        write_tail(msg_ref, state[...], t_ref[0:1, :])


def local_z_kernel(u2_ref, s_ref, b_t_ref, c_ref, r_ref, ends_ref, y_ref, mask, state):
    step = pl.program_id(0)

    @pl.when(step == 0)
    def _():
        mask[...] = spread_mask()
        state[...] = jnp.zeros_like(state)

    here = slab_at(step)
    u2s = [u2_ref[chunk_rows(at), :] for at in range(PER)]
    scores = [s_ref[chunk_rows(at), :] for at in range(PER)]
    b_ts = [b_t_ref[:, chunk_rows(at)] for at in range(PER)]
    cs = [c_ref[chunk_rows(at), :] for at in range(PER)]
    slabs = (ends_ref[0, here, :], ends_ref[1, here, :], ends_ref[2, here, :])
    local_scan(u2s, scores, b_ts, cs, slabs, r_ref[here, :], mask[...], state, y_ref)


def gate_z_kernel(y_ref, c_ref, gate_ref, r_ref, e_ref, got_ref, out_ref, state, mask):
    step = pl.program_id(0)

    @pl.when(step == 0)
    def _():
        start_state(got_ref, state)
        mask[...] = spread_mask()

    def write(at, value):
        gate = gate_ref[chunk_rows(at), :].astype(F32)
        silu = gate / (1.0 + jnp.exp(-gate))
        out_ref[chunk_rows(at), :] = (value.astype(BF16).astype(F32) * silu).astype(BF16)

    here = slab_at(step)
    add_start(y_ref, c_ref, r_ref[here, :], e_ref[here, :], mask[...], state, write)


def final_kernel(x_ref, w_ref, out_ref):
    parts = [x_ref[k].astype(F32) for k in range(8)]
    squares = sum(part * part for part in parts)
    mean = jnp.sum(squares, axis=1, keepdims=True) * (1.0 / 1024.0)
    scale = lax.rsqrt(mean + 1e-05)
    total = None
    for k in range(8):
        parts3 = w_ref[k, LANES:TAIL, 0:LANES].astype(F32)
        gain = parts3[0:1] + parts3[1:2] + parts3[2:3]
        term = mm((parts[k] * scale * gain).astype(BF16), w_ref[k, 0:LANES, :])
        total = term if total is None else total + term
    out_ref[...] = total.astype(BF16)


ROW = (STEP, LANES)
FLAT = (CHUNK, LANES)
GOT_X = (GROUPS, MSG, LANES)
GOT_Z = (GROUPS, TAIL, LANES)
ENDS = (3, CHUNK, LANES)
MASK = pltpu.VMEM((48, STEP), BF16)
STATE = pltpu.VMEM(FLAT, F32)


def block(shape, index):
    return pl.BlockSpec(shape, index)


def fixed(shape):
    return pl.BlockSpec(shape, lambda *_: (0,) * len(shape))


def each(i, *_):
    return (i, 0)


def early(i, *_):
    return (jnp.minimum(i, STEPS - 1), 0)


def late(i, *_):
    return (jnp.maximum(i - STEPS, 0), 0)


def struct(shape, dtype):
    return jax.ShapeDtypeStruct(shape, dtype)


def call(kernel, name, steps, ins, outs, shapes, scratch, mib, prefetch=0, limit=56):
    return pl.pallas_call(
        kernel,
        name=name,
        grid_spec=pltpu.PrefetchScalarGridSpec(
            num_scalar_prefetch=prefetch, grid=(steps,), in_specs=ins, out_specs=outs, scratch_shapes=scratch
        ),
        out_shape=shapes,
        compiler_params=pltpu.CompilerParams(
            dimension_semantics=("arbitrary",), vmem_limit_bytes=limit * 1024 * 1024
        ),
        cost_estimate=pl.CostEstimate(flops=mib << 28, bytes_accessed=mib << 20, transcendentals=0),
    )


def states_x(g, d, b, u):
    return call(
        states_x_kernel, "states_x", STEPS,
        [fixed(FLAT), fixed(FLAT), block(ROW, each), block(ROW, each)],
        fixed((TAIL, LANES)), struct((TAIL, LANES), BF16),
        [STATE, MASK, STATE, pltpu.VMEM((8, LANES), F32)], 4,
    )(g, d, b, u)


def local_x(g, d, b, c, u):
    return call(
        local_x_kernel, "local_x", STEPS,
        [fixed(FLAT), fixed(FLAT), block(ROW, each), block(ROW, each), block(ROW, each)],
        [block(ROW, each), fixed(FLAT), fixed(FLAT)],
        [struct((TOK, LANES), F32), struct(FLAT, F32), struct(FLAT, F32)],
        [STATE, pltpu.VMEM(ENDS, F32), MASK, STATE], 10,
    )(g, d, b, c, u)


def send_x(y, c, r, e, got):
    return call(
        send_x_kernel, "send_x", 2 * STEPS,
        [block(ROW, early), block(ROW, early), fixed(FLAT), fixed(FLAT), fixed(GOT_X)],
        block(ROW, late), struct((TOK, LANES), BF16),
        [
            STATE, MASK, pltpu.VMEM(ROW, F32), pltpu.VMEM((TOK, LANES), F32),
            pltpu.VMEM((64, LANES), jnp.int32), pltpu.SMEM((64, LANES), jnp.int32), pltpu.SemaphoreType.DMA,
        ], 10,
    )(y, c, r, e, got)


def before_z(g, d, b, c):
    return call(
        before_z_kernel, "before_z", STEPS,
        [fixed(FLAT), fixed(FLAT), block(ROW, each), block(ROW, each)],
        [
            block(ROW, each), block((CHUNK, STEP), lambda i: (0, i)), fixed(FLAT), fixed((8, LANES)),
            fixed(FLAT), fixed(FLAT), fixed(FLAT), fixed(ENDS),
        ],
        [
            struct((TOK, LANES), BF16), struct((CHUNK, TOK), BF16), struct(FLAT, F32), struct((8, LANES), F32),
            struct(FLAT, F32), struct(FLAT, F32), struct(FLAT, F32), struct(ENDS, F32),
        ],
        [], 8,
    )(g, d, b, c)


def states_z(place, w, t, a, b_t, got):
    return call(
        states_z_kernel, "states_z", 2 * STEPS,
        [
            fixed(FLAT), fixed((8, LANES)), fixed(FLAT),
            block((CHUNK, STEP), lambda i, _: (0, jnp.maximum(i - STEPS, 0))), block(ROW, early),
        ],
        [block(ROW, late), fixed((TAIL, LANES))],
        [struct((TOK, LANES), BF16), struct((TAIL, LANES), BF16)],
        [MASK, STATE, pltpu.VMEM(ROW, F32), pltpu.VMEM((TOK, LANES), F32)], 8, prefetch=1,
    )(place, w, t, a, b_t, got)


def local_z(u2, s, b_t, c, r, ends):
    return call(
        local_z_kernel, "local_z", STEPS,
        [
            block(ROW, each), block(ROW, each), block((CHUNK, STEP), lambda i: (0, i)), block(ROW, each),
            fixed(FLAT), fixed(ENDS),
        ],
        block(ROW, each), struct((TOK, LANES), F32), [MASK, STATE], 10,
    )(u2, s, b_t, c, r, ends)


def gate_z(y, c, gate, r, e, got):
    return call(
        gate_z_kernel, "gate_z", STEPS,
        [block(ROW, each), block(ROW, each), block(ROW, each), fixed(FLAT), fixed(FLAT), fixed(GOT_Z)],
        block(ROW, each), struct((TOK, LANES), BF16), [STATE, MASK], 10,
    )(y, c, gate, r, e, got)


def final(x, w):
    rows = 256
    return call(
        final_kernel, "final", 1024 // rows,
        [block((8, rows, LANES), lambda i: (0, i, 0)), fixed((8, TAIL, 512))],
        block((rows, 512), each), struct((1024, 512), BF16), [], 5,
    )(x, w)


def three_pieces(value):
    high = lax.reduce_precision(value, 8, 7)
    mid = lax.reduce_precision(value - high, 8, 7)
    return high, mid, value - high - mid


def flat(value):
    return value.reshape(2, TOK // CHUNK, CHUNK).transpose(1, 0, 2).reshape(CHUNK, LANES)


def body(
    x_inputs,
    x_in_proj,
    x_out_proj,
    x_log_decay,
    x_step,
    z_source,
    z_in_proj,
    z_out_proj,
    z_log_decay,
    z_step,
    gate_branch,
    norm_gain,
    out_weight,
):
    order = jnp.sort(z_source * TOK + lax.iota(jnp.int32, TOK))
    place = order & (TOK - 1)
    source = (order >> 13) & (TOK - 1)
    lists = jnp.concatenate(
        [(source >> 7).reshape(GROUPS, 4, LANES), (source & 127).reshape(GROUPS, 4, LANES)], axis=1
    ).astype(BF16)

    gain = jnp.pad(jnp.stack(three_pieces(norm_gain)), ((0, TAIL - LANES - 3), (0, 512 - LANES))).astype(BF16)
    weights = lax.all_gather(jnp.concatenate([out_weight, gain], axis=0), "head", axis=0, tiled=False)

    g_x, d_x = flat(x_log_decay), flat(x_step)
    tail_x = states_x(g_x, d_x, x_in_proj, x_inputs)
    message = jnp.concatenate([jnp.broadcast_to(tail_x[None], GOT_Z), lists], axis=1)
    message, g_x, d_x = lax.optimization_barrier((message, g_x, d_x))
    got_x = lax.all_to_all(message, "seq", 0, 0)
    y_x, r_x, e_x = local_x(g_x, d_x, x_in_proj, x_out_proj, x_inputs)
    sent = send_x(y_x, x_out_proj, r_x, e_x, got_x)
    sent, g_z, d_z = lax.optimization_barrier((sent, z_log_decay, z_step))
    received = lax.all_to_all(sent.reshape(GROUPS, PIECE, LANES), "seq", 0, 0).reshape(TOK, LANES)
    s_z, b_t, w_z, t_z, a_z, r_z, e_z, ends_z = before_z(flat(g_z), flat(d_z), z_in_proj, z_out_proj)
    u2_z, tail_z = states_z(place, w_z, t_z, a_z, b_t, received)
    got_z = lax.all_to_all(jnp.broadcast_to(tail_z[None], GOT_Z), "seq", 0, 0)
    y_z = local_z(u2_z, s_z, b_t, z_out_proj, r_z, ends_z)
    gated = gate_z(y_z, z_out_proj, gate_branch, r_z, e_z, got_z)
    whole = lax.all_to_all(gated.reshape(8, 1024, LANES), "head", 0, 0)
    return final(whole, weights)


def solution(mesh):
    placed = (
        P("seq", "head"),
        P("seq", None),
        P("seq", None),
        P("head", "seq"),
        P("head", "seq"),
        P("seq"),
        P("seq", None),
        P("seq", None),
        P("head", "seq"),
        P("head", "seq"),
        P("seq", "head"),
        P("head"),
        P("head", None),
    )
    return jax.shard_map(
        body, mesh=mesh, in_specs=placed, out_specs=P(("seq", "head"), None), check_vma=False
    )
```

```python
import functools

import jax
import jax.numpy as jnp
from jax import lax
from jax.experimental import pallas as pl
from jax.experimental.pallas import tpu as pltpu
from jax.sharding import PartitionSpec as P

TOK = 8192
LANES = 128
CHUNK = 128
STEP = 4096
PER = STEP // CHUNK
STEPS = TOK // STEP
PIECE = 512
GROUPS = 16
TAIL = 144
MSG = 160
WROWS = 136
F32 = jnp.float32
BF16 = jnp.bfloat16


def mm(a, b):
    return jnp.dot(a, b, preferred_element_type=F32)


def nt(a, b):
    return lax.dot_general(a, b, (((1,), (1,)), ((), ())), preferred_element_type=F32)


def tn(a, b):
    return lax.dot_general(a, b, (((0,), (0,)), ((), ())), preferred_element_type=F32)


def iotas():
    shape = (CHUNK, CHUNK)
    return lax.broadcasted_iota(jnp.int32, shape, 0), lax.broadcasted_iota(jnp.int32, shape, 1)


def ones(condition):
    return jnp.where(condition, 1.0, 0.0).astype(BF16)


def pieces(value, axis):
    high = value.astype(BF16)
    rest = value - high.astype(F32)
    mid = rest.astype(BF16)
    low = (rest - mid.astype(F32)).astype(BF16)
    return jnp.concatenate([high, mid, low], axis=axis)


def thrice(mask, axis):
    return jnp.concatenate([mask, mask, mask], axis=axis)


def wide(column):
    return jnp.broadcast_to(column, (CHUNK, LANES))


def by_head(first, second):
    return jnp.where(lax.broadcasted_iota(jnp.int32, (1, LANES), 1) < 64, first, second)


def row_pair(slab, at):
    return by_head(slab[2 * at : 2 * at + 1], slab[2 * at + 1 : 2 * at + 2])


def spread_mask():
    row = lax.broadcasted_iota(jnp.int32, (6 * PER, STEP), 0) & (2 * PER - 1)
    col = lax.broadcasted_iota(jnp.int32, (6 * PER, STEP), 1)
    return ones(row == 2 * (col >> 7) + ((col >> 6) & 1))


def spread(slab, mask):
    return tn(pieces(slab, 0), mask)


def slab_at(step):
    return pl.ds(pl.multiple_of(2 * PER * step, 2 * PER), 2 * PER)


def end_weights(g, d):
    row, col = iotas()
    inner = mm(pieces(g, 1), thrice(ones(row > col), 0))
    total = wide(inner[:, 0:1] + g[:, 0:1])
    later = mm(thrice(ones((col > row) & ((col & 1) == (row & 1))), 1), pieces(total, 0))
    whole = later[0:2] + total[0:2]
    return jnp.exp(inner + later) * d, by_head(whole[0:1], whole[1:2])


def scan_factors(g, d):
    row, col = iotas()
    cum = mm(pieces(g, 1), thrice(ones(row <= col), 0))
    mid = wide(cum[:, CHUNK // 2 - 1 : CHUNK // 2])
    total = wide(cum[:, CHUNK - 1 : CHUNK])
    before = mm(thrice(ones((col < row) & ((col & 1) == (row & 1))), 1), pieces(total, 0))
    return (
        jnp.exp(mid - cum) * d,
        jnp.exp(cum - mid),
        jnp.exp(mid),
        jnp.exp(total),
        jnp.exp(total - mid),
        jnp.exp(mid + before),
    )


def write_tail(msg_ref, state, total):
    high = total.astype(BF16).astype(F32)
    mid = (total - high).astype(BF16).astype(F32)
    low = total - high - mid
    pad = jnp.zeros((TAIL - CHUNK - 3, LANES), F32)
    tail = jnp.concatenate([state, high, mid, low, pad], axis=0).astype(BF16)
    for k in range(GROUPS):
        msg_ref[k, 0:TAIL, :] = tail


def match_rows(index, count):
    return lax.broadcasted_iota(jnp.int32, (count, LANES), 0) == index


def route(z_ref, msg_ref, place_ref):
    z = z_ref[...]
    group, token = z >> 13, z & (TOK - 1)
    row, col = iotas()
    hits = [group == k for k in range(GROUPS)]
    inside = mm(jnp.concatenate([ones(hit) for hit in hits], axis=0), ones(row <= col))
    counts = [inside[64 * k : 64 * k + 64] for k in range(GROUPS)]
    sums = jnp.concatenate([jnp.broadcast_to(count[:, 127:128], (64, LANES)) for count in counts], axis=1)
    above = mm(ones(row > col)[0:64, 0:64], sums.astype(BF16))
    slot = jnp.zeros((64, LANES), F32)
    for k in range(GROUPS):
        rank = counts[k] + above[:, k * LANES : (k + 1) * LANES] + float(k * PIECE - 1)
        slot = jnp.where(hits[k], rank, slot)
    slot = slot.astype(jnp.int32)
    slot_high, slot_low = slot >> 7, slot & 127
    token_high, token_low = (token >> 7).astype(F32), (token & 127).astype(F32)
    lane = lax.broadcasted_iota(jnp.int32, (1, LANES), 1).astype(F32)
    total = jnp.zeros((256, LANES), F32)
    for base in range(0, 64, 4):
        lefts, rights = [], []
        for q in range(base, base + 4):
            hit = match_rows(slot_high[q : q + 1], 64)
            values = (token_high[q : q + 1], token_low[q : q + 1], float(q), lane)
            lefts.append(jnp.concatenate([jnp.where(hit, value, 0.0) for value in values], axis=0).astype(BF16))
            rights.append(ones(match_rows(slot_low[q : q + 1], LANES)))
        total = total + nt(jnp.concatenate(lefts, axis=1), jnp.concatenate(rights, axis=1))
    place_ref[...] = (total[128:192] * 128.0 + total[192:256]).astype(jnp.int32)
    for k in range(GROUPS):
        rows = slice(4 * k, 4 * k + 4)
        wanted = jnp.concatenate([total[rows], total[64 + 4 * k : 68 + 4 * k], jnp.zeros((8, LANES), F32)], axis=0)
        msg_ref[k, TAIL:MSG, :] = wanted.astype(BF16)


def chunk_rows(at):
    return slice(at * CHUNK, (at + 1) * CHUNK)


def states_x_kernel(z_ref, g_ref, d_ref, b_ref, u_ref, msg_ref, place_ref, weights, mask, state, total):
    step = pl.program_id(0)

    @pl.when(step == 0)
    def _():
        route(z_ref, msg_ref, place_ref)
        weights[...], total[0:1, :] = end_weights(g_ref[...], d_ref[...])
        mask[...] = spread_mask()
        state[...] = jnp.zeros_like(state)

    scale = spread(weights[slab_at(step), :], mask[...])
    parts = [
        (u_ref[chunk_rows(at), :].astype(F32) * scale[:, chunk_rows(at)]).astype(BF16) for at in range(PER)
    ]
    state[...] += tn(b_ref[...], jnp.concatenate(parts, axis=0))

    @pl.when(step == STEPS - 1)
    def _():
        write_tail(msg_ref, state[...], total[0:1, :])


def local_scan(u2s, scores, b_ts, cs, slabs, r_slab, mask, state, y_ref):
    into, end, add = slabs
    carry = state[...]
    sums = [mm(b_ts[at], u2s[at]) for at in range(PER)]
    helds = []
    for at in range(PER):
        helds.append((carry * row_pair(into, at)).astype(BF16))
        carry = row_pair(end, at) * carry + row_pair(add, at) * sums[at]
    state[...] = carry
    back = spread(r_slab, mask)
    for at in range(PER):
        left = jnp.concatenate([scores[at], cs[at]], axis=1)
        right = jnp.concatenate([u2s[at], helds[at]], axis=0)
        y_ref[chunk_rows(at), :] = back[:, chunk_rows(at)] * mm(left, right)


def local_x_kernel(g_ref, d_ref, b_ref, c_ref, u_ref, y_ref, r_ref, e_ref, a_all, ends, mask, state):
    step = pl.program_id(0)

    @pl.when(step == 0)
    def _():
        a_all[...], r_ref[...], ends[0], ends[1], ends[2], e_ref[...] = scan_factors(g_ref[...], d_ref[...])
        mask[...] = spread_mask()
        state[...] = jnp.zeros_like(state)

    row, col = iotas()
    lower = row >= col
    here = slab_at(step)
    scale = spread(a_all[here, :], mask[...])
    u2s = [(u_ref[chunk_rows(at), :].astype(F32) * scale[:, chunk_rows(at)]).astype(BF16) for at in range(PER)]
    b_ts = [b_ref[chunk_rows(at), :].T for at in range(PER)]
    cs = [c_ref[chunk_rows(at), :] for at in range(PER)]
    scores = [jnp.where(lower, mm(cs[at], b_ts[at]), 0.0).astype(BF16) for at in range(PER)]
    slabs = (ends[0, here, :], ends[1, here, :], ends[2, here, :])
    local_scan(u2s, scores, b_ts, cs, slabs, r_ref[here, :], mask[...], state, y_ref)


def start_state(got_ref, state):
    me = lax.axis_index("seq")
    state[...] = jnp.zeros_like(state)
    for k in range(GROUPS - 1):

        @pl.when(k < me)
        def _():
            tail = got_ref[k, CHUNK:TAIL, :].astype(F32)
            decay = jnp.exp(tail[0:1] + tail[1:2] + tail[2:3])
            state[...] = decay * state[...] + got_ref[k, 0:CHUNK, :].astype(F32)


def add_start(y_ref, c_ref, r_slab, e_slab, mask, state, write):
    back = spread(r_slab, mask)
    start = state[...]
    for at in range(PER):
        held = (start * row_pair(e_slab, at)).astype(BF16)
        write(at, y_ref[chunk_rows(at), :] + back[:, chunk_rows(at)] * mm(c_ref[chunk_rows(at), :], held))


def invert_lists(got_ref, slots):
    high = lax.broadcasted_iota(jnp.int32, (64, LANES), 0).astype(F32)
    low = lax.broadcasted_iota(jnp.int32, (LANES, LANES), 0).astype(F32)
    lane = lax.broadcasted_iota(jnp.int32, (64, LANES), 1).astype(F32)
    total = jnp.zeros((LANES, LANES), F32)
    for k in range(GROUPS):
        lists = got_ref[k, TAIL:MSG, :].astype(F32)
        lefts, rights = [], []
        for q in range(4):
            hit = high == lists[q : q + 1]
            lefts.append(
                jnp.concatenate([jnp.where(hit, float(4 * k + q), 0.0), jnp.where(hit, lane, 0.0)], axis=0).astype(BF16)
            )
            rights.append(ones(low == lists[4 + q : 5 + q]))
        total = total + nt(jnp.concatenate(lefts, axis=1), jnp.concatenate(rights, axis=1))
    slots[...] = (total[0:64] * 128.0 + total[64:128]).astype(jnp.int32)


def scatter(rows, table, line, ordered):
    def put(i, _):
        for q in range(LANES // 8):
            value = rows[pl.ds(pl.multiple_of(i * LANES + q * 8, 8), 8), :]
            for k in range(8):
                ordered[pl.ds(table[line + i, q * 8 + k], 1), :] = value[k : k + 1, :]
        return 0

    lax.fori_loop(0, PER, put, 0)


def send_x_kernel(
    y_ref, c_ref, r_ref, e_ref, got_ref, out_ref, state, mask, rows, ordered, slots, table, sem
):
    step = pl.program_id(0)

    @pl.when(step == 0)
    def _():
        invert_lists(got_ref, slots)
        copy = pltpu.make_async_copy(slots, table, sem)
        copy.start()
        start_state(got_ref, state)
        mask[...] = spread_mask()
        copy.wait()

    @pl.when(step < STEPS)
    def _():
        here = slab_at(step)

        def write(at, value):
            rows[chunk_rows(at), :] = value

        add_start(y_ref, c_ref, r_ref[here, :], e_ref[here, :], mask[...], state, write)

        scatter(rows, table, step * PER, ordered)

    @pl.when(step >= STEPS)
    def _():
        base = pl.multiple_of((step - STEPS) * STEP, STEP)
        out_ref[...] = ordered[pl.ds(base, STEP), :].astype(BF16)


def before_z_kernel(
    g_ref, d_ref, b_ref, c_ref, s_ref, b_t_ref, w_ref, t_ref, a_ref, r_ref, e_ref, ends_ref
):
    @pl.when(pl.program_id(0) == 0)
    def _():
        w_ref[...], total = end_weights(g_ref[...], d_ref[...])
        t_ref[...] = jnp.broadcast_to(total, (8, LANES))
        a_ref[...], r_ref[...], ends_ref[0], ends_ref[1], ends_ref[2], e_ref[...] = scan_factors(
            g_ref[...], d_ref[...]
        )

    row, col = iotas()
    lower = row >= col
    for at in range(PER):
        b_t = b_ref[chunk_rows(at), :].T
        b_t_ref[:, chunk_rows(at)] = b_t
        s_ref[chunk_rows(at), :] = jnp.where(lower, mm(c_ref[chunk_rows(at), :], b_t), 0.0).astype(BF16)


def states_z_kernel(place, w_ref, t_ref, a_ref, b_t_ref, got_ref, u2_ref, msg_ref, mask, state, rows, ordered):
    step = pl.program_id(0)

    @pl.when(step == 0)
    def _():
        mask[...] = spread_mask()
        state[...] = jnp.zeros_like(state)

    @pl.when(step < STEPS)
    def _():
        rows[...] = got_ref[...].astype(F32)

        scatter(rows, place, step * PER, ordered)

    @pl.when(step >= STEPS)
    def _():
        base = (step - STEPS) * STEP
        here = slab_at(step - STEPS)
        weight = spread(w_ref[here, :], mask[...])
        scale = spread(a_ref[here, :], mask[...])
        parts = []
        for at in range(PER):
            u = ordered[pl.ds(pl.multiple_of(base + at * CHUNK, CHUNK), CHUNK), :]
            u2_ref[chunk_rows(at), :] = (u * scale[:, chunk_rows(at)]).astype(BF16)
            parts.append((u * weight[:, chunk_rows(at)]).astype(BF16))
        state[...] += mm(b_t_ref[...], jnp.concatenate(parts, axis=0))

    @pl.when(step == 2 * STEPS - 1)
    def _():
        write_tail(msg_ref, state[...], t_ref[0:1, :])


def local_z_kernel(u2_ref, s_ref, b_t_ref, c_ref, r_ref, ends_ref, y_ref, mask, state):
    step = pl.program_id(0)

    @pl.when(step == 0)
    def _():
        mask[...] = spread_mask()
        state[...] = jnp.zeros_like(state)

    here = slab_at(step)
    u2s = [u2_ref[chunk_rows(at), :] for at in range(PER)]
    scores = [s_ref[chunk_rows(at), :] for at in range(PER)]
    b_ts = [b_t_ref[:, chunk_rows(at)] for at in range(PER)]
    cs = [c_ref[chunk_rows(at), :] for at in range(PER)]
    slabs = (ends_ref[0, here, :], ends_ref[1, here, :], ends_ref[2, here, :])
    local_scan(u2s, scores, b_ts, cs, slabs, r_ref[here, :], mask[...], state, y_ref)


def gate_z_kernel(y_ref, c_ref, gate_ref, r_ref, e_ref, got_ref, out_ref, state, mask):
    step = pl.program_id(0)

    @pl.when(step == 0)
    def _():
        start_state(got_ref, state)
        mask[...] = spread_mask()

    def write(at, value):
        gate = gate_ref[chunk_rows(at), :].astype(F32)
        silu = gate * (0.5 * jnp.tanh(0.5 * gate) + 0.5)
        out_ref[chunk_rows(at), :] = (value.astype(BF16).astype(F32) * silu).astype(BF16)

    here = slab_at(step)
    add_start(y_ref, c_ref, r_ref[here, :], e_ref[here, :], mask[...], state, write)


def final_kernel(x_ref, w_ref, out_ref):
    parts = [x_ref[k].astype(F32) for k in range(8)]
    squares = sum(part * part for part in parts)
    mean = jnp.sum(squares, axis=1, keepdims=True) * (1.0 / 1024.0)
    scale = lax.rsqrt(mean + 1e-05)
    total = None
    for k in range(8):
        parts3 = w_ref[k, LANES:WROWS, 0:LANES].astype(F32)
        gain = parts3[0:1] + parts3[1:2] + parts3[2:3]
        term = mm((parts[k] * scale * gain).astype(BF16), w_ref[k, 0:LANES, :])
        total = term if total is None else total + term
    out_ref[...] = total.astype(BF16)


ROW = (STEP, LANES)
FLAT = (CHUNK, LANES)
GOT_X = (GROUPS, MSG, LANES)
GOT_Z = (GROUPS, TAIL, LANES)
ENDS = (3, CHUNK, LANES)
MASK = pltpu.VMEM((6 * PER, STEP), BF16)
STATE = pltpu.VMEM(FLAT, F32)


def block(shape, index):
    return pl.BlockSpec(shape, index)


def fixed(shape):
    return pl.BlockSpec(shape, lambda *_: (0,) * len(shape))


def each(i, *_):
    return (i, 0)


def early(i, *_):
    return (jnp.minimum(i, STEPS - 1), 0)


def late(i, *_):
    return (jnp.maximum(i - STEPS, 0), 0)


def struct(shape, dtype):
    return jax.ShapeDtypeStruct(shape, dtype)


def call(kernel, name, steps, ins, outs, shapes, scratch, mib, prefetch=0, limit=56):
    return pl.pallas_call(
        kernel,
        name=name,
        grid_spec=pltpu.PrefetchScalarGridSpec(
            num_scalar_prefetch=prefetch, grid=(steps,), in_specs=ins, out_specs=outs, scratch_shapes=scratch
        ),
        out_shape=shapes,
        compiler_params=pltpu.CompilerParams(
            dimension_semantics=("arbitrary",), vmem_limit_bytes=limit * 1024 * 1024
        ),
        cost_estimate=pl.CostEstimate(flops=mib << 28, bytes_accessed=mib << 20, transcendentals=0),
    )


def states_x(z, g, d, b, u):
    return call(
        states_x_kernel, "states_x", STEPS,
        [fixed((64, LANES)), fixed(FLAT), fixed(FLAT), block(ROW, each), block(ROW, each)],
        [fixed(GOT_X), fixed((64, LANES))], [struct(GOT_X, BF16), struct((64, LANES), jnp.int32)],
        [STATE, MASK, STATE, pltpu.VMEM((8, LANES), F32)], 4,
    )(z, g, d, b, u)


def local_x(g, d, b, c, u):
    return call(
        local_x_kernel, "local_x", STEPS,
        [fixed(FLAT), fixed(FLAT), block(ROW, each), block(ROW, each), block(ROW, each)],
        [block(ROW, each), fixed(FLAT), fixed(FLAT)],
        [struct((TOK, LANES), F32), struct(FLAT, F32), struct(FLAT, F32)],
        [STATE, pltpu.VMEM(ENDS, F32), MASK, STATE], 10,
    )(g, d, b, c, u)


def send_x(y, c, r, e, got):
    return call(
        send_x_kernel, "send_x", 2 * STEPS,
        [block(ROW, early), block(ROW, early), fixed(FLAT), fixed(FLAT), fixed(GOT_X)],
        block(ROW, late), struct((TOK, LANES), BF16),
        [
            STATE, MASK, pltpu.VMEM(ROW, F32), pltpu.VMEM((TOK, LANES), F32),
            pltpu.VMEM((64, LANES), jnp.int32), pltpu.SMEM((64, LANES), jnp.int32), pltpu.SemaphoreType.DMA,
        ], 10,
    )(y, c, r, e, got)


def before_z(g, d, b, c):
    return call(
        before_z_kernel, "before_z", STEPS,
        [fixed(FLAT), fixed(FLAT), block(ROW, each), block(ROW, each)],
        [
            block(ROW, each), block((CHUNK, STEP), lambda i: (0, i)), fixed(FLAT), fixed((8, LANES)),
            fixed(FLAT), fixed(FLAT), fixed(FLAT), fixed(ENDS),
        ],
        [
            struct((TOK, LANES), BF16), struct((CHUNK, TOK), BF16), struct(FLAT, F32), struct((8, LANES), F32),
            struct(FLAT, F32), struct(FLAT, F32), struct(FLAT, F32), struct(ENDS, F32),
        ],
        [], 8,
    )(g, d, b, c)


def states_z(place, w, t, a, b_t, got):
    return call(
        states_z_kernel, "states_z", 2 * STEPS,
        [
            fixed(FLAT), fixed((8, LANES)), fixed(FLAT),
            block((CHUNK, STEP), lambda i, _: (0, jnp.maximum(i - STEPS, 0))), block(ROW, early),
        ],
        [block(ROW, late), fixed(GOT_Z)],
        [struct((TOK, LANES), BF16), struct(GOT_Z, BF16)],
        [MASK, STATE, pltpu.VMEM(ROW, F32), pltpu.VMEM((TOK, LANES), F32)], 8, prefetch=1,
    )(place, w, t, a, b_t, got)


def local_z(u2, s, b_t, c, r, ends):
    return call(
        local_z_kernel, "local_z", STEPS,
        [
            block(ROW, each), block(ROW, each), block((CHUNK, STEP), lambda i: (0, i)), block(ROW, each),
            fixed(FLAT), fixed(ENDS),
        ],
        block(ROW, each), struct((TOK, LANES), F32), [MASK, STATE], 10,
    )(u2, s, b_t, c, r, ends)


def gate_z(y, c, gate, r, e, got):
    return call(
        gate_z_kernel, "gate_z", STEPS,
        [block(ROW, each), block(ROW, each), block(ROW, each), fixed(FLAT), fixed(FLAT), fixed(GOT_Z)],
        block(ROW, each), struct((TOK, LANES), BF16), [STATE, MASK], 10,
    )(y, c, gate, r, e, got)


def final(x, w):
    rows = 256
    return call(
        final_kernel, "final", 1024 // rows,
        [block((8, rows, LANES), lambda i: (0, i, 0)), fixed((8, WROWS, 512))],
        block((rows, 512), each), struct((1024, 512), BF16), [], 5, limit=20,
    )(x, w)


def three_pieces(value):
    high = lax.reduce_precision(value, 8, 7)
    mid = lax.reduce_precision(value - high, 8, 7)
    return high, mid, value - high - mid


def flat(value):
    return value.reshape(2, TOK // CHUNK, CHUNK).transpose(1, 0, 2).reshape(CHUNK, LANES)


def body(
    x_inputs,
    x_in_proj,
    x_out_proj,
    x_log_decay,
    x_step,
    z_source,
    z_in_proj,
    z_out_proj,
    z_log_decay,
    z_step,
    gate_branch,
    norm_gain,
    out_weight,
):
    g_x, d_x = flat(x_log_decay), flat(x_step)
    message, place = states_x(z_source.reshape(64, LANES), g_x, d_x, x_in_proj, x_inputs)
    message, g_x, d_x = lax.optimization_barrier((message, g_x, d_x))
    got_x = lax.all_to_all(message, "seq", 0, 0)
    y_x, r_x, e_x = local_x(g_x, d_x, x_in_proj, x_out_proj, x_inputs)
    sent = send_x(y_x, x_out_proj, r_x, e_x, got_x)
    sent, g_z, d_z, norm_gain, out_weight = lax.optimization_barrier(
        (sent, z_log_decay, z_step, norm_gain, out_weight)
    )
    gain = jnp.pad(jnp.stack(three_pieces(norm_gain)), ((0, WROWS - LANES - 3), (0, 512 - LANES))).astype(BF16)
    weights = lax.all_gather(jnp.concatenate([out_weight, gain], axis=0), "head", axis=0, tiled=False)
    received = lax.all_to_all(sent.reshape(GROUPS, PIECE, LANES), "seq", 0, 0).reshape(TOK, LANES)
    s_z, b_t, w_z, t_z, a_z, r_z, e_z, ends_z = before_z(flat(g_z), flat(d_z), z_in_proj, z_out_proj)
    u2_z, tails_z = states_z(place, w_z, t_z, a_z, b_t, received)
    got_z = lax.all_to_all(tails_z, "seq", 0, 0)
    y_z = local_z(u2_z, s_z, b_t, z_out_proj, r_z, ends_z)
    gated = gate_z(y_z, z_out_proj, gate_branch, r_z, e_z, got_z)
    whole = lax.all_to_all(gated.reshape(8, 1024, LANES), "head", 0, 0)
    return final(whole, weights)


def solution(mesh):
    placed = (
        P("seq", "head"),
        P("seq", None),
        P("seq", None),
        P("head", "seq"),
        P("head", "seq"),
        P("seq"),
        P("seq", None),
        P("seq", None),
        P("head", "seq"),
        P("head", "seq"),
        P("seq", "head"),
        P("head"),
        P("head", None),
    )
    return jax.shard_map(
        body, mesh=mesh, in_specs=placed, out_specs=P(("seq", "head"), None), check_vma=False
    )
```

```python
import math

import jax
import jax.numpy as jnp
from jax import lax
from jax.experimental import pallas as pl
from jax.experimental.pallas import tpu as pltpu
from jax.sharding import PartitionSpec as P

TOK = 8192
LANES = 128
CHUNK = 128
STEP = 4096
PER = STEP // CHUNK
STEPS = TOK // STEP
PIECE = 512
GROUPS = 16
TAIL = 144
MSG = 160
WROWS = 136
F32 = jnp.float32
BF16 = jnp.bfloat16


def mm(a, b):
    return jnp.dot(a, b, preferred_element_type=F32)


def nt(a, b):
    return lax.dot_general(a, b, (((1,), (1,)), ((), ())), preferred_element_type=F32)


def tn(a, b):
    return lax.dot_general(a, b, (((0,), (0,)), ((), ())), preferred_element_type=F32)


def iotas():
    shape = (CHUNK, CHUNK)
    return lax.broadcasted_iota(jnp.int32, shape, 0), lax.broadcasted_iota(jnp.int32, shape, 1)


def ones(condition):
    return jnp.where(condition, 1.0, 0.0).astype(BF16)


def pieces(value, axis):
    high = value.astype(BF16)
    rest = value - high.astype(F32)
    mid = rest.astype(BF16)
    low = (rest - mid.astype(F32)).astype(BF16)
    return jnp.concatenate([high, mid, low], axis=axis)


def thrice(mask, axis):
    return jnp.concatenate([mask, mask, mask], axis=axis)


def wide(column):
    return jnp.broadcast_to(column, (CHUNK, LANES))


def by_head(first, second):
    return jnp.where(lax.broadcasted_iota(jnp.int32, (1, LANES), 1) < 64, first, second)


def row_pair(slab, at):
    return by_head(slab[2 * at : 2 * at + 1], slab[2 * at + 1 : 2 * at + 2])


def spread_mask():
    row = lax.broadcasted_iota(jnp.int32, (6 * PER, STEP), 0) & (2 * PER - 1)
    col = lax.broadcasted_iota(jnp.int32, (6 * PER, STEP), 1)
    return ones(row == 2 * (col >> 7) + ((col >> 6) & 1))


def spread(slab, mask):
    return tn(pieces(slab, 0), mask)


def slab_at(step):
    return pl.ds(pl.multiple_of(2 * PER * step, 2 * PER), 2 * PER)


def end_weights(g, d):
    row, col = iotas()
    inner = mm(pieces(g, 1), thrice(ones(row > col), 0))
    total = wide(inner[:, 0:1] + g[:, 0:1])
    later = mm(thrice(ones((col > row) & ((col & 1) == (row & 1))), 1), pieces(total, 0))
    whole = later[0:2] + total[0:2]
    return jnp.exp(inner + later) * d, by_head(whole[0:1], whole[1:2])


def scan_factors(g, d):
    row, col = iotas()
    cum = mm(pieces(g, 1), thrice(ones(row <= col), 0))
    mid = wide(cum[:, CHUNK // 2 - 1 : CHUNK // 2])
    total = wide(cum[:, CHUNK - 1 : CHUNK])
    same = (col & 1) == (row & 1)
    before = mm(thrice(ones((col < row) & same), 1), pieces(total, 0))
    after = mm(thrice(ones((col > row) & same), 1), pieces(total, 0))
    return (
        jnp.exp(mid - cum) * d,
        jnp.exp(cum - mid),
        jnp.exp(mid),
        jnp.exp(total),
        jnp.exp(total - mid),
        jnp.exp(mid + before),
        jnp.exp(total - mid + after),
    )


def write_tail(msg_ref, state, total):
    high = total.astype(BF16).astype(F32)
    mid = (total - high).astype(BF16).astype(F32)
    low = total - high - mid
    pad = jnp.zeros((TAIL - CHUNK - 3, LANES), F32)
    tail = jnp.concatenate([state, high, mid, low, pad], axis=0).astype(BF16)
    for k in range(GROUPS):
        msg_ref[k, 0:TAIL, :] = tail


def match_rows(index, count):
    return lax.broadcasted_iota(jnp.int32, (count, LANES), 0) == index


def route(z_ref, msg_ref, place_ref):
    z = z_ref[...]
    group, token = z >> 13, z & (TOK - 1)
    row, col = iotas()
    hits = [group == k for k in range(GROUPS)]
    inside = mm(jnp.concatenate([ones(hit) for hit in hits], axis=0), ones(row <= col))
    counts = [inside[64 * k : 64 * k + 64] for k in range(GROUPS)]
    sums = jnp.concatenate([jnp.broadcast_to(count[:, 127:128], (64, LANES)) for count in counts], axis=1)
    above = mm(ones(row > col)[0:64, 0:64], sums.astype(BF16))
    slot = jnp.zeros((64, LANES), F32)
    for k in range(GROUPS):
        rank = counts[k] + above[:, k * LANES : (k + 1) * LANES] + float(k * PIECE - 1)
        slot = jnp.where(hits[k], rank, slot)
    slot = slot.astype(jnp.int32)
    slot_high, slot_low = slot >> 7, slot & 127
    token_high, token_low = (token >> 7).astype(F32), (token & 127).astype(F32)
    lane = lax.broadcasted_iota(jnp.int32, (1, LANES), 1).astype(F32)
    total = jnp.zeros((256, LANES), F32)
    for base in range(0, 64, 4):
        lefts, rights = [], []
        for q in range(base, base + 4):
            hit = match_rows(slot_high[q : q + 1], 64)
            values = (token_high[q : q + 1], token_low[q : q + 1], float(q), lane)
            lefts.append(jnp.concatenate([jnp.where(hit, value, 0.0) for value in values], axis=0).astype(BF16))
            rights.append(ones(match_rows(slot_low[q : q + 1], LANES)))
        total = total + nt(jnp.concatenate(lefts, axis=1), jnp.concatenate(rights, axis=1))
    place_ref[...] = (total[128:192] * 128.0 + total[192:256]).astype(jnp.int32)
    for k in range(GROUPS):
        rows = slice(4 * k, 4 * k + 4)
        wanted = jnp.concatenate([total[rows], total[64 + 4 * k : 68 + 4 * k], jnp.zeros((8, LANES), F32)], axis=0)
        msg_ref[k, TAIL:MSG, :] = wanted.astype(BF16)


def chunk_rows(at):
    return slice(at * CHUNK, (at + 1) * CHUNK)


def states_x_kernel(z_ref, g_ref, d_ref, b_ref, u_ref, msg_ref, place_ref, weights, mask, state, total):
    step = pl.program_id(0)

    @pl.when(step == 0)
    def _():
        route(z_ref, msg_ref, place_ref)
        weights[...], total[0:1, :] = end_weights(g_ref[...], d_ref[...])
        mask[...] = spread_mask()
        state[...] = jnp.zeros_like(state)

    scale = spread(weights[slab_at(step), :], mask[...])
    parts = [
        (u_ref[chunk_rows(at), :].astype(F32) * scale[:, chunk_rows(at)]).astype(BF16) for at in range(PER)
    ]
    state[...] += tn(b_ref[...], jnp.concatenate(parts, axis=0))

    @pl.when(step == STEPS - 1)
    def _():
        write_tail(msg_ref, state[...], total[0:1, :])


def local_scan(u2s, scores, b_ts, cs, slabs, state, finish):
    into, end, add = slabs
    carry = state[...]
    sums = [mm(b_ts[at], u2s[at]) for at in range(PER)]
    helds = []
    for at in range(PER):
        helds.append((carry * row_pair(into, at)).astype(BF16))
        carry = row_pair(end, at) * carry + row_pair(add, at) * sums[at]
    state[...] = carry
    for at in range(PER):
        left = jnp.concatenate([scores[at], cs[at]], axis=1)
        right = jnp.concatenate([u2s[at], helds[at]], axis=0)
        finish(at, mm(left, right))


def local_x_kernel(g_ref, d_ref, b_ref, c_ref, u_ref, y_ref, back_ref, e_ref, a_all, r_all, ends, mask, state):
    step = pl.program_id(0)

    @pl.when(step == 0)
    def _():
        a_all[...], r_all[...], ends[0], ends[1], ends[2], e_ref[...], _ = scan_factors(g_ref[...], d_ref[...])
        mask[...] = spread_mask()
        state[...] = jnp.zeros_like(state)

    row, col = iotas()
    lower = row >= col
    here = slab_at(step)
    scale = spread(a_all[here, :], mask[...])
    u2s = [(u_ref[chunk_rows(at), :].astype(F32) * scale[:, chunk_rows(at)]).astype(BF16) for at in range(PER)]
    b_ts = [b_ref[chunk_rows(at), :].T for at in range(PER)]
    cs = [c_ref[chunk_rows(at), :] for at in range(PER)]
    scores = [jnp.where(lower, mm(cs[at], b_ts[at]), 0.0).astype(BF16) for at in range(PER)]
    slabs = (ends[0, here, :], ends[1, here, :], ends[2, here, :])

    back = spread(r_all[here, :], mask[...])

    def finish(at, value):
        y_ref[chunk_rows(at), :] = back[:, chunk_rows(at)] * value
        back_ref[chunk_rows(at), :] = back[:, chunk_rows(at)]

    local_scan(u2s, scores, b_ts, cs, slabs, state, finish)


def start_state(got_ref, state):
    me = lax.axis_index("seq")
    state[...] = jnp.zeros_like(state)
    for k in range(GROUPS - 1):

        @pl.when(k < me)
        def _():
            tail = got_ref[k, CHUNK:TAIL, :].astype(F32)
            decay = jnp.exp(tail[0:1] + tail[1:2] + tail[2:3])
            state[...] = decay * state[...] + got_ref[k, 0:CHUNK, :].astype(F32)


def add_start(y_ref, c_ref, back_ref, e_slab, state, out_ref):
    start = state[...]
    for at in range(PER):
        rows = chunk_rows(at)
        held = (start * row_pair(e_slab, at)).astype(BF16)
        value = y_ref[rows, :] + back_ref[rows, :] * mm(c_ref[rows, :], held)
        out_ref[rows, :] = value.astype(out_ref.dtype)


def invert_lists(got_ref, slots):
    high = lax.broadcasted_iota(jnp.int32, (64, LANES), 0).astype(F32)
    low = lax.broadcasted_iota(jnp.int32, (LANES, LANES), 0).astype(F32)
    lane = lax.broadcasted_iota(jnp.int32, (64, LANES), 1).astype(F32)
    total = jnp.zeros((LANES, LANES), F32)
    for k in range(GROUPS):
        lists = got_ref[k, TAIL:MSG, :].astype(F32)
        lefts, rights = [], []
        for q in range(4):
            hit = high == lists[q : q + 1]
            lefts.append(
                jnp.concatenate([jnp.where(hit, float(4 * k + q), 0.0), jnp.where(hit, lane, 0.0)], axis=0).astype(BF16)
            )
            rights.append(ones(low == lists[4 + q : 5 + q]))
        total = total + nt(jnp.concatenate(lefts, axis=1), jnp.concatenate(rights, axis=1))
    slots[...] = (total[0:64] * 128.0 + total[64:128]).astype(jnp.int32)


def scatter(rows, table, line, ordered):
    def put(i, _):
        for q in range(LANES // 8):
            value = rows[pl.ds(pl.multiple_of(i * LANES + q * 8, 8), 8), :]
            for k in range(8):
                ordered[pl.ds(table[line + i, q * 8 + k], 1), :] = value[k : k + 1, :]
        return 0

    lax.fori_loop(0, PER, put, 0)


def send_x_kernel(
    y_ref, c_ref, back_ref, e_ref, got_ref, out_ref, state, rows, ordered, slots, table, sem
):
    step = pl.program_id(0)

    @pl.when(step == 0)
    def _():
        invert_lists(got_ref, slots)
        copy = pltpu.make_async_copy(slots, table, sem)
        copy.start()
        start_state(got_ref, state)
        copy.wait()

    @pl.when(step < STEPS)
    def _():
        add_start(y_ref, c_ref, back_ref, e_ref[slab_at(step), :], state, rows)
        scatter(rows, table, step * PER, ordered)

    @pl.when(step >= STEPS)
    def _():
        base = pl.multiple_of((step - STEPS) * STEP, STEP)
        out_ref[...] = ordered[pl.ds(base, STEP), :].astype(BF16)


def before_z_kernel(
    g_ref, d_ref, b_ref, c_ref, gate_ref,
    s_ref, b_t_ref, scale_ref, back_ref, t_ref, f_ref, e_ref, ends_ref, a_all, r_all, mask,
):
    step = pl.program_id(0)

    @pl.when(step == 0)
    def _():
        _, total = end_weights(g_ref[...], d_ref[...])
        t_ref[...] = jnp.broadcast_to(total, (8, LANES))
        a_all[...], r_all[...], ends_ref[0], ends_ref[1], ends_ref[2], e_ref[...], f_ref[...] = scan_factors(
            g_ref[...], d_ref[...]
        )
        mask[...] = spread_mask()

    row, col = iotas()
    lower = row >= col
    here = slab_at(step)
    scale = spread(a_all[here, :], mask[...])
    back = spread(r_all[here, :], mask[...])
    for at in range(PER):
        rows = chunk_rows(at)
        b_t = b_ref[rows, :].T
        b_t_ref[:, rows] = b_t
        s_ref[rows, :] = jnp.where(lower, mm(c_ref[rows, :], b_t), 0.0).astype(BF16)
        scale_ref[rows, :] = scale[:, rows]
        gate = gate_ref[rows, :].astype(F32)
        silu = gate * (0.5 * jnp.tanh(0.5 * gate) + 0.5)
        back_ref[rows, :] = silu * back[:, rows]


def states_z_kernel(place, t_ref, f_ref, scale_ref, b_t_ref, got_ref, u2_ref, msg_ref, state, rows, ordered):
    step = pl.program_id(0)

    @pl.when(step == 0)
    def _():
        state[...] = jnp.zeros_like(state)

    @pl.when(step < STEPS)
    def _():
        rows[...] = got_ref[...].astype(F32)
        scatter(rows, place, step * PER, ordered)

    @pl.when(step >= STEPS)
    def _():
        base = (step - STEPS) * STEP
        factor = f_ref[slab_at(step - STEPS), :]
        u2s = []
        for at in range(PER):
            here = chunk_rows(at)
            u = ordered[pl.ds(pl.multiple_of(base + at * CHUNK, CHUNK), CHUNK), :]
            u2 = (u * scale_ref[here, :]).astype(BF16)
            u2_ref[here, :] = u2
            u2s.append(u2)
        total = state[...]
        for at in range(PER):
            total = total + row_pair(factor, at) * mm(b_t_ref[:, chunk_rows(at)], u2s[at])
        state[...] = total

    @pl.when(step == 2 * STEPS - 1)
    def _():
        write_tail(msg_ref, state[...], t_ref[0:1, :])


def local_z_kernel(u2_ref, s_ref, b_t_ref, c_ref, back_ref, ends_ref, y_ref, state):
    step = pl.program_id(0)

    @pl.when(step == 0)
    def _():
        state[...] = jnp.zeros_like(state)

    here = slab_at(step)
    u2s = [u2_ref[chunk_rows(at), :] for at in range(PER)]
    scores = [s_ref[chunk_rows(at), :] for at in range(PER)]
    b_ts = [b_t_ref[:, chunk_rows(at)] for at in range(PER)]
    cs = [c_ref[chunk_rows(at), :] for at in range(PER)]
    slabs = (ends_ref[0, here, :], ends_ref[1, here, :], ends_ref[2, here, :])

    def finish(at, value):
        y_ref[chunk_rows(at), :] = back_ref[chunk_rows(at), :] * value

    local_scan(u2s, scores, b_ts, cs, slabs, state, finish)


def gate_z_kernel(y_ref, c_ref, back_ref, e_ref, got_ref, out_ref, state):
    step = pl.program_id(0)

    @pl.when(step == 0)
    def _():
        start_state(got_ref, state)

    add_start(y_ref, c_ref, back_ref, e_ref[slab_at(step), :], state, out_ref)


def final_kernel(x_ref, w_ref, out_ref):
    parts = [x_ref[k].astype(F32) for k in range(8)]
    squares = sum(part * part for part in parts)
    mean = jnp.sum(squares, axis=1, keepdims=True) * (1.0 / 1024.0)
    scale = lax.rsqrt(mean + 1e-05)
    total = None
    for k in range(8):
        parts3 = w_ref[k, LANES:WROWS, 0:LANES].astype(F32)
        gain = parts3[0:1] + parts3[1:2] + parts3[2:3]
        term = mm((parts[k] * scale * gain).astype(BF16), w_ref[k, 0:LANES, :])
        total = term if total is None else total + term
    out_ref[...] = total.astype(BF16)


ROW = (STEP, LANES)
FLAT = (CHUNK, LANES)
GOT_X = (GROUPS, MSG, LANES)
GOT_Z = (GROUPS, TAIL, LANES)
ENDS = (3, CHUNK, LANES)
MASK = pltpu.VMEM((6 * PER, STEP), BF16)
STATE = pltpu.VMEM(FLAT, F32)


def block(shape, index):
    return pl.BlockSpec(shape, index)


def fixed(shape):
    return pl.BlockSpec(shape, lambda *_: (0,) * len(shape))


def each(i, *_):
    return (i, 0)


def early(i, *_):
    return (jnp.minimum(i, STEPS - 1), 0)


def late(i, *_):
    return (jnp.maximum(i - STEPS, 0), 0)


def struct(shape, dtype):
    return jax.ShapeDtypeStruct(shape, dtype)


def call(kernel, name, steps, ins, outs, shapes, scratch, mib, prefetch=0, limit=36, loose=-1):
    large = 1 << 13
    shapes = jax.tree.map(
        lambda shape: pltpu.HBM(shape.shape, shape.dtype) if math.prod(shape.shape) >= large else shape, shapes
    )
    made = pl.pallas_call(
        kernel,
        name=name,
        grid_spec=pltpu.PrefetchScalarGridSpec(
            num_scalar_prefetch=prefetch, grid=(steps,), in_specs=ins, out_specs=outs, scratch_shapes=scratch
        ),
        out_shape=shapes,
        compiler_params=pltpu.CompilerParams(
            dimension_semantics=("arbitrary",), vmem_limit_bytes=limit * 1024 * 1024
        ),
        cost_estimate=pl.CostEstimate(flops=mib << 28, bytes_accessed=mib << 20, transcendentals=0),
    )

    def run(*values):
        return made(
            *[
                pltpu.with_memory_space_constraint(value, pltpu.HBM)
                if at != loose and value.size >= large
                else value
                for at, value in enumerate(values)
            ]
        )

    return run


def states_x(z, g, d, b, u):
    return call(
        states_x_kernel, "states_x", STEPS,
        [fixed((64, LANES)), fixed(FLAT), fixed(FLAT), block(ROW, each), block(ROW, each)],
        [fixed(GOT_X), fixed((64, LANES))], [struct(GOT_X, BF16), struct((64, LANES), jnp.int32)],
        [STATE, MASK, STATE, pltpu.VMEM((8, LANES), F32)], 4,
    )(z, g, d, b, u)


def local_x(g, d, b, c, u):
    return call(
        local_x_kernel, "local_x", STEPS,
        [fixed(FLAT), fixed(FLAT), block(ROW, each), block(ROW, each), block(ROW, each)],
        [block(ROW, each), block(ROW, each), fixed(FLAT)],
        [struct((TOK, LANES), F32), struct((TOK, LANES), F32), struct(FLAT, F32)],
        [STATE, STATE, pltpu.VMEM(ENDS, F32), MASK, STATE], 12,
    )(g, d, b, c, u)


def send_x(y, c, back, e, got):
    return call(
        send_x_kernel, "send_x", 2 * STEPS,
        [block(ROW, early), block(ROW, early), block(ROW, early), fixed(FLAT), fixed(GOT_X)],
        block(ROW, late), struct((TOK, LANES), BF16),
        [
            STATE, pltpu.VMEM(ROW, F32), pltpu.VMEM((TOK, LANES), F32),
            pltpu.VMEM((64, LANES), jnp.int32), pltpu.SMEM((64, LANES), jnp.int32), pltpu.SemaphoreType.DMA,
        ], 12, loose=4,
    )(y, c, back, e, got)


def before_z(g, d, b, c, gate):
    return call(
        before_z_kernel, "before_z", STEPS,
        [fixed(FLAT), fixed(FLAT), block(ROW, each), block(ROW, each), block(ROW, each)],
        [
            block(ROW, each), block((CHUNK, STEP), lambda i: (0, i)), block(ROW, each), block(ROW, each),
            fixed((8, LANES)), fixed(FLAT), fixed(FLAT), fixed(ENDS),
        ],
        [
            struct((TOK, LANES), BF16), struct((CHUNK, TOK), BF16), struct((TOK, LANES), F32),
            struct((TOK, LANES), F32), struct((8, LANES), F32), struct(FLAT, F32), struct(FLAT, F32),
            struct(ENDS, F32),
        ],
        [STATE, STATE, MASK], 18,
    )(g, d, b, c, gate)


def states_z(place, t, f, scale, b_t, got):
    return call(
        states_z_kernel, "states_z", 2 * STEPS,
        [
            fixed((8, LANES)), fixed(FLAT), block(ROW, late),
            block((CHUNK, STEP), lambda i, _: (0, jnp.maximum(i - STEPS, 0))), block(ROW, early),
        ],
        [block(ROW, late), fixed(GOT_Z)],
        [struct((TOK, LANES), BF16), struct(GOT_Z, BF16)],
        [STATE, pltpu.VMEM(ROW, F32), pltpu.VMEM((TOK, LANES), F32)], 10, prefetch=1, loose=5,
    )(place, t, f, scale, b_t, got)


def local_z(u2, s, b_t, c, back, ends):
    return call(
        local_z_kernel, "local_z", STEPS,
        [
            block(ROW, each), block(ROW, each), block((CHUNK, STEP), lambda i: (0, i)), block(ROW, each),
            block(ROW, each), fixed(ENDS),
        ],
        block(ROW, each), struct((TOK, LANES), F32), [STATE], 14,
    )(u2, s, b_t, c, back, ends)


def gate_z(y, c, back, e, got):
    return call(
        gate_z_kernel, "gate_z", STEPS,
        [block(ROW, each), block(ROW, each), block(ROW, each), fixed(FLAT), fixed(GOT_Z)],
        block(ROW, each), struct((TOK, LANES), BF16), [STATE], 12, loose=4,
    )(y, c, back, e, got)


def final(x, w):
    rows = 256
    return call(
        final_kernel, "final", 1024 // rows,
        [block((8, rows, LANES), lambda i: (0, i, 0)), fixed((8, WROWS, 512))],
        block((rows, 512), each), struct((1024, 512), BF16), [], 5, limit=20, loose=0,
    )(x, w)


def three_pieces(value):
    high = lax.reduce_precision(value, 8, 7)
    mid = lax.reduce_precision(value - high, 8, 7)
    return high, mid, value - high - mid


def flat(value):
    return value.reshape(2, TOK // CHUNK, CHUNK).transpose(1, 0, 2).reshape(CHUNK, LANES)


def body(
    x_inputs,
    x_in_proj,
    x_out_proj,
    x_log_decay,
    x_step,
    z_source,
    z_in_proj,
    z_out_proj,
    z_log_decay,
    z_step,
    gate_branch,
    norm_gain,
    out_weight,
):
    g_x, d_x = flat(x_log_decay), flat(x_step)
    message, place = states_x(z_source.reshape(64, LANES), g_x, d_x, x_in_proj, x_inputs)
    message, g_x, d_x = lax.optimization_barrier((message, g_x, d_x))
    got_x = lax.all_to_all(message, "seq", 0, 0)
    y_x, back_x, e_x = local_x(g_x, d_x, x_in_proj, x_out_proj, x_inputs)
    sent = send_x(y_x, x_out_proj, back_x, e_x, got_x)
    sent, g_z, d_z, norm_gain, out_weight = lax.optimization_barrier(
        (sent, z_log_decay, z_step, norm_gain, out_weight)
    )
    gain = jnp.pad(jnp.stack(three_pieces(norm_gain)), ((0, WROWS - LANES - 3), (0, 512 - LANES))).astype(BF16)
    weights = lax.all_gather(jnp.concatenate([out_weight, gain], axis=0), "head", axis=0, tiled=False)
    received = lax.all_to_all(sent.reshape(GROUPS, PIECE, LANES), "seq", 0, 0).reshape(TOK, LANES)
    s_z, b_t, scale_z, back_z, t_z, f_z, e_z, ends_z = before_z(
        flat(g_z), flat(d_z), z_in_proj, z_out_proj, gate_branch
    )
    received, weights = lax.optimization_barrier((received, weights))
    u2_z, tails_z = states_z(place, t_z, f_z, scale_z, b_t, received)
    got_z = lax.all_to_all(tails_z, "seq", 0, 0)
    y_z = local_z(u2_z, s_z, b_t, z_out_proj, back_z, ends_z)
    gated = gate_z(y_z, z_out_proj, back_z, e_z, got_z)
    whole = lax.all_to_all(gated.reshape(8, 1024, LANES), "head", 0, 0)
    return final(whole, weights)


def solution(mesh):
    placed = (
        P("seq", "head"),
        P("seq", None),
        P("seq", None),
        P("head", "seq"),
        P("head", "seq"),
        P("seq"),
        P("seq", None),
        P("seq", None),
        P("head", "seq"),
        P("head", "seq"),
        P("seq", "head"),
        P("head"),
        P("head", None),
    )
    return jax.shard_map(
        body, mesh=mesh, in_specs=placed, out_specs=P(("seq", "head"), None), check_vma=False
    )
```

```python
import math

import jax
import jax.numpy as jnp
from jax import lax
from jax.experimental import pallas as pl
from jax.experimental.pallas import tpu as pltpu
from jax.sharding import PartitionSpec as P

TOK = 8192
LANES = 128
CHUNK = 128
STEP = 4096
PER = STEP // CHUNK
STEPS = TOK // STEP
PIECE = 512
GROUPS = 16
TAIL = 144
MSG = 160
WROWS = 136
TOGETHER = 16
F32 = jnp.float32
BF16 = jnp.bfloat16


def mm(a, b):
    return jnp.dot(a, b, preferred_element_type=F32)


def nt(a, b):
    return lax.dot_general(a, b, (((1,), (1,)), ((), ())), preferred_element_type=F32)


def tn(a, b):
    return lax.dot_general(a, b, (((0,), (0,)), ((), ())), preferred_element_type=F32)


def iotas():
    shape = (CHUNK, CHUNK)
    return lax.broadcasted_iota(jnp.int32, shape, 0), lax.broadcasted_iota(jnp.int32, shape, 1)


def ones(condition):
    return jnp.where(condition, 1.0, 0.0).astype(BF16)


def pieces(value, axis):
    high = value.astype(BF16)
    rest = value - high.astype(F32)
    mid = rest.astype(BF16)
    low = (rest - mid.astype(F32)).astype(BF16)
    return jnp.concatenate([high, mid, low], axis=axis)


def thrice(mask, axis):
    return jnp.concatenate([mask, mask, mask], axis=axis)


def wide(column):
    return jnp.broadcast_to(column, (CHUNK, LANES))


def by_head(first, second):
    return jnp.where(lax.broadcasted_iota(jnp.int32, (1, LANES), 1) < 64, first, second)


def row_pair(slab, at):
    return by_head(slab[2 * at : 2 * at + 1], slab[2 * at + 1 : 2 * at + 2])


def spread_mask():
    row = lax.broadcasted_iota(jnp.int32, (6 * PER, STEP), 0) & (2 * PER - 1)
    col = lax.broadcasted_iota(jnp.int32, (6 * PER, STEP), 1)
    return ones(row == 2 * (col >> 7) + ((col >> 6) & 1))


def spread(slab, mask):
    return tn(pieces(slab, 0), mask)


def slab_at(step):
    return pl.ds(pl.multiple_of(2 * PER * step, 2 * PER), 2 * PER)


def end_weights(g, d):
    row, col = iotas()
    inner = mm(pieces(g, 1), thrice(ones(row > col), 0))
    total = wide(inner[:, 0:1] + g[:, 0:1])
    later = mm(thrice(ones((col > row) & ((col & 1) == (row & 1))), 1), pieces(total, 0))
    whole = later[0:2] + total[0:2]
    return jnp.exp(inner + later) * d, by_head(whole[0:1], whole[1:2])


def scan_factors(g, d):
    row, col = iotas()
    cum = mm(pieces(g, 1), thrice(ones(row <= col), 0))
    mid = wide(cum[:, CHUNK // 2 - 1 : CHUNK // 2])
    total = wide(cum[:, CHUNK - 1 : CHUNK])
    same = (col & 1) == (row & 1)
    before = mm(thrice(ones((col < row) & same), 1), pieces(total, 0))
    after = mm(thrice(ones((col > row) & same), 1), pieces(total, 0))
    return (
        jnp.exp(mid - cum) * d,
        jnp.exp(cum - mid),
        jnp.exp(mid),
        jnp.exp(total),
        jnp.exp(total - mid),
        jnp.exp(mid + before),
        jnp.exp(total - mid + after),
    )


def write_tail(msg_ref, state, total):
    high = total.astype(BF16).astype(F32)
    mid = (total - high).astype(BF16).astype(F32)
    low = total - high - mid
    pad = jnp.zeros((TAIL - CHUNK - 3, LANES), F32)
    tail = jnp.concatenate([state, high, mid, low, pad], axis=0).astype(BF16)
    for k in range(GROUPS):
        msg_ref[k, 0:TAIL, :] = tail


def match_rows(index, count):
    return lax.broadcasted_iota(jnp.int32, (count, LANES), 0) == index


def route(z_ref, msg_ref, place_ref):
    z = z_ref[...]
    group, token = z >> 13, z & (TOK - 1)
    row, col = iotas()
    hits = [group == k for k in range(GROUPS)]
    inside = mm(jnp.concatenate([ones(hit) for hit in hits], axis=0), ones(row <= col))
    counts = [inside[64 * k : 64 * k + 64] for k in range(GROUPS)]
    sums = jnp.concatenate([jnp.broadcast_to(count[:, 127:128], (64, LANES)) for count in counts], axis=1)
    above = mm(ones(row > col)[0:64, 0:64], sums.astype(BF16))
    slot = jnp.zeros((64, LANES), F32)
    for k in range(GROUPS):
        rank = counts[k] + above[:, k * LANES : (k + 1) * LANES] + float(k * PIECE - 1)
        slot = jnp.where(hits[k], rank, slot)
    slot = slot.astype(jnp.int32)
    place_ref[...] = slot
    slot_high, slot_low = slot >> 7, slot & 127
    token_high, token_low = (token >> 7).astype(F32), (token & 127).astype(F32)
    total = jnp.zeros((LANES, LANES), F32)
    for base in range(0, 64, 4):
        lefts, rights = [], []
        for q in range(base, base + 4):
            hit = match_rows(slot_high[q : q + 1], 64)
            values = (token_high[q : q + 1], token_low[q : q + 1])
            lefts.append(jnp.concatenate([jnp.where(hit, value, 0.0) for value in values], axis=0).astype(BF16))
            rights.append(ones(match_rows(slot_low[q : q + 1], LANES)))
        total = total + nt(jnp.concatenate(lefts, axis=1), jnp.concatenate(rights, axis=1))
    for k in range(GROUPS):
        rows = slice(4 * k, 4 * k + 4)
        wanted = jnp.concatenate([total[rows], total[64 + 4 * k : 68 + 4 * k], jnp.zeros((8, LANES), F32)], axis=0)
        msg_ref[k, TAIL:MSG, :] = wanted.astype(BF16)


def chunk_rows(at):
    return slice(at * CHUNK, (at + 1) * CHUNK)


def states_x_kernel(z_ref, g_ref, d_ref, b_ref, u_ref, msg_ref, place_ref, weights, mask, state, total):
    step = pl.program_id(0)

    @pl.when(step == 0)
    def _():
        route(z_ref, msg_ref, place_ref)
        weights[...], total[0:1, :] = end_weights(g_ref[...], d_ref[...])
        mask[...] = spread_mask()
        state[...] = jnp.zeros_like(state)

    scale = spread(weights[slab_at(step), :], mask[...])
    parts = [
        (u_ref[chunk_rows(at), :].astype(F32) * scale[:, chunk_rows(at)]).astype(BF16) for at in range(PER)
    ]
    state[...] += tn(b_ref[...], jnp.concatenate(parts, axis=0))

    @pl.when(step == STEPS - 1)
    def _():
        write_tail(msg_ref, state[...], total[0:1, :])


def local_scan(u2s, scores, b_ts, cs, slabs, state, finish):
    into, end, add = slabs
    carry = state[...]
    sums = [mm(b_ts[at], u2s[at]) for at in range(PER)]
    helds = []
    for at in range(PER):
        helds.append((carry * row_pair(into, at)).astype(BF16))
        carry = row_pair(end, at) * carry + row_pair(add, at) * sums[at]
    state[...] = carry
    for at in range(PER):
        left = jnp.concatenate([scores[at], cs[at]], axis=1)
        right = jnp.concatenate([u2s[at], helds[at]], axis=0)
        finish(at, mm(left, right))


def local_x_kernel(g_ref, d_ref, b_ref, c_ref, u_ref, y_ref, back_ref, e_ref, a_all, r_all, ends, mask, state):
    step = pl.program_id(0)

    @pl.when(step == 0)
    def _():
        a_all[...], r_all[...], ends[0], ends[1], ends[2], e_ref[...], _ = scan_factors(g_ref[...], d_ref[...])
        mask[...] = spread_mask()
        state[...] = jnp.zeros_like(state)

    row, col = iotas()
    lower = row >= col
    here = slab_at(step)
    scale = spread(a_all[here, :], mask[...])
    u2s = [(u_ref[chunk_rows(at), :].astype(F32) * scale[:, chunk_rows(at)]).astype(BF16) for at in range(PER)]
    b_ts = [b_ref[chunk_rows(at), :].T for at in range(PER)]
    cs = [c_ref[chunk_rows(at), :] for at in range(PER)]
    scores = [jnp.where(lower, mm(cs[at], b_ts[at]), 0.0).astype(BF16) for at in range(PER)]
    slabs = (ends[0, here, :], ends[1, here, :], ends[2, here, :])

    back = spread(r_all[here, :], mask[...])

    def finish(at, value):
        y_ref[chunk_rows(at), :] = back[:, chunk_rows(at)] * value
        back_ref[chunk_rows(at), :] = back[:, chunk_rows(at)]

    local_scan(u2s, scores, b_ts, cs, slabs, state, finish)


def start_state(got_ref, state):
    me = lax.axis_index("seq")
    state[...] = jnp.zeros_like(state)
    for k in range(GROUPS - 1):

        @pl.when(k < me)
        def _():
            tail = got_ref[k, CHUNK:TAIL, :].astype(F32)
            decay = jnp.exp(tail[0:1] + tail[1:2] + tail[2:3])
            state[...] = decay * state[...] + got_ref[k, 0:CHUNK, :].astype(F32)


def add_start(y_ref, c_ref, back_ref, e_slab, state, out_ref, base=0):
    start = state[...]
    for at in range(PER):
        rows = chunk_rows(at)
        held = (start * row_pair(e_slab, at)).astype(BF16)
        value = y_ref[rows, :] + back_ref[rows, :] * mm(c_ref[rows, :], held)
        out_ref[pl.ds(pl.multiple_of(base + at * CHUNK, CHUNK), CHUNK), :] = value.astype(out_ref.dtype)


def read_lists(got_ref, slots):
    for k in range(GROUPS):
        lists = got_ref[k, TAIL:MSG, :].astype(F32)
        slots[4 * k : 4 * k + 4, :] = (lists[0:4] * 128.0 + lists[4:8]).astype(jnp.int32)


def take_rows(source, table, line, first, count):
    return jnp.concatenate([source[pl.ds(table[line, first + k], 1), :] for k in range(count)], axis=0)


def send_x_kernel(
    y_ref, c_ref, back_ref, e_ref, got_ref, out_ref, state, rows, slots, table, sem
):
    step = pl.program_id(0)

    @pl.when(step == 0)
    def _():
        read_lists(got_ref, slots)
        copy = pltpu.make_async_copy(slots, table, sem)
        copy.start()
        start_state(got_ref, state)
        copy.wait()

    @pl.when(step < STEPS)
    def _():
        base = step * STEP
        add_start(y_ref, c_ref, back_ref, e_ref[slab_at(step), :], state, rows, base)

    @pl.when(step >= STEPS)
    def _():
        def take(i, _):
            for q in range(LANES // 16):
                here = pl.ds(pl.multiple_of(i * LANES + q * 16, 16), 16)
                out_ref[here, :] = take_rows(rows, table, (step - STEPS) * PER + i, q * 16, 16).astype(BF16)
            return 0

        lax.fori_loop(0, PER, take, 0)


def before_z_kernel(
    g_ref, d_ref, b_ref, c_ref, gate_ref,
    s_ref, b_t_ref, scale_ref, back_ref, t_ref, f_ref, e_ref, ends_ref, a_all, r_all, mask,
):
    step = pl.program_id(0)

    @pl.when(step == 0)
    def _():
        _, total = end_weights(g_ref[...], d_ref[...])
        t_ref[...] = jnp.broadcast_to(total, (8, LANES))
        a_all[...], r_all[...], ends_ref[0], ends_ref[1], ends_ref[2], e_ref[...], f_ref[...] = scan_factors(
            g_ref[...], d_ref[...]
        )
        mask[...] = spread_mask()

    row, col = iotas()
    lower = row >= col
    here = slab_at(step)
    scale = spread(a_all[here, :], mask[...])
    back = spread(r_all[here, :], mask[...])
    for at in range(PER):
        rows = chunk_rows(at)
        b_t = b_ref[rows, :].T
        b_t_ref[:, rows] = b_t
        s_ref[rows, :] = jnp.where(lower, mm(c_ref[rows, :], b_t), 0.0).astype(BF16)
        scale_ref[rows, :] = scale[:, rows]
        gate = gate_ref[rows, :].astype(F32)
        silu = gate * (0.5 * jnp.tanh(0.5 * gate) + 0.5)
        back_ref[rows, :] = silu * back[:, rows]


def states_z_kernel(place, t_ref, f_ref, scale_ref, b_t_ref, got_ref, u2_ref, msg_ref, state, rows):
    step = pl.program_id(0)

    @pl.when(step == 0)
    def _():
        state[...] = jnp.zeros_like(state)

    @pl.when(step < STEPS)
    def _():
        rows[pl.ds(pl.multiple_of(step * STEP, STEP), STEP), :] = got_ref[...].astype(F32)

    @pl.when(step >= STEPS)
    def _():
        block_at = step - STEPS

        def one(i, total):
            for at in range(TOGETHER):
                chunk = i * TOGETHER + at
                here = pl.ds(pl.multiple_of(chunk * CHUNK, CHUNK), CHUNK)
                line = block_at * PER + chunk
                u = take_rows(rows, place, line, 0, CHUNK)
                u2 = (u * scale_ref[here, :]).astype(BF16)
                u2_ref[here, :] = u2
                factor = by_head(f_ref[pl.ds(2 * line, 1), :], f_ref[pl.ds(2 * line + 1, 1), :])
                total = total + factor * mm(b_t_ref[:, here], u2)
            return total

        state[...] = lax.fori_loop(0, PER // TOGETHER, one, state[...])

    @pl.when(step == 2 * STEPS - 1)
    def _():
        write_tail(msg_ref, state[...], t_ref[0:1, :])


def local_z_kernel(u2_ref, s_ref, b_t_ref, c_ref, back_ref, ends_ref, y_ref, state):
    step = pl.program_id(0)

    @pl.when(step == 0)
    def _():
        state[...] = jnp.zeros_like(state)

    here = slab_at(step)
    u2s = [u2_ref[chunk_rows(at), :] for at in range(PER)]
    scores = [s_ref[chunk_rows(at), :] for at in range(PER)]
    b_ts = [b_t_ref[:, chunk_rows(at)] for at in range(PER)]
    cs = [c_ref[chunk_rows(at), :] for at in range(PER)]
    slabs = (ends_ref[0, here, :], ends_ref[1, here, :], ends_ref[2, here, :])

    def finish(at, value):
        y_ref[chunk_rows(at), :] = back_ref[chunk_rows(at), :] * value

    local_scan(u2s, scores, b_ts, cs, slabs, state, finish)


def gate_z_kernel(y_ref, c_ref, back_ref, e_ref, got_ref, out_ref, state):
    step = pl.program_id(0)

    @pl.when(step == 0)
    def _():
        start_state(got_ref, state)

    add_start(y_ref, c_ref, back_ref, e_ref[slab_at(step), :], state, out_ref)


def final_kernel(x_ref, w_ref, out_ref):
    parts = [x_ref[k].astype(F32) for k in range(8)]
    squares = sum(part * part for part in parts)
    mean = jnp.sum(squares, axis=1, keepdims=True) * (1.0 / 1024.0)
    scale = lax.rsqrt(mean + 1e-05)
    total = None
    for k in range(8):
        parts3 = w_ref[k, LANES:WROWS, 0:LANES].astype(F32)
        gain = parts3[0:1] + parts3[1:2] + parts3[2:3]
        term = mm((parts[k] * scale * gain).astype(BF16), w_ref[k, 0:LANES, :])
        total = term if total is None else total + term
    out_ref[...] = total.astype(BF16)


ROW = (STEP, LANES)
FLAT = (CHUNK, LANES)
GOT_X = (GROUPS, MSG, LANES)
GOT_Z = (GROUPS, TAIL, LANES)
ENDS = (3, CHUNK, LANES)
MASK = pltpu.VMEM((6 * PER, STEP), BF16)
STATE = pltpu.VMEM(FLAT, F32)


def block(shape, index):
    return pl.BlockSpec(shape, index)


def fixed(shape):
    return pl.BlockSpec(shape, lambda *_: (0,) * len(shape))


def each(i, *_):
    return (i, 0)


def early(i, *_):
    return (jnp.minimum(i, STEPS - 1), 0)


def late(i, *_):
    return (jnp.maximum(i - STEPS, 0), 0)


def struct(shape, dtype):
    return jax.ShapeDtypeStruct(shape, dtype)


def call(kernel, name, steps, ins, outs, shapes, scratch, mib, prefetch=0, limit=36, loose=-1):
    large = 1 << 13
    shapes = jax.tree.map(
        lambda shape: pltpu.HBM(shape.shape, shape.dtype) if math.prod(shape.shape) >= large else shape, shapes
    )
    made = pl.pallas_call(
        kernel,
        name=name,
        grid_spec=pltpu.PrefetchScalarGridSpec(
            num_scalar_prefetch=prefetch, grid=(steps,), in_specs=ins, out_specs=outs, scratch_shapes=scratch
        ),
        out_shape=shapes,
        compiler_params=pltpu.CompilerParams(
            dimension_semantics=("arbitrary",), vmem_limit_bytes=limit * 1024 * 1024
        ),
        cost_estimate=pl.CostEstimate(flops=mib << 28, bytes_accessed=mib << 20, transcendentals=0),
    )

    def run(*values):
        return made(
            *[
                pltpu.with_memory_space_constraint(value, pltpu.HBM)
                if at != loose and value.size >= large
                else value
                for at, value in enumerate(values)
            ]
        )

    return run


def states_x(z, g, d, b, u):
    return call(
        states_x_kernel, "states_x", STEPS,
        [fixed((64, LANES)), fixed(FLAT), fixed(FLAT), block(ROW, each), block(ROW, each)],
        [fixed(GOT_X), fixed((64, LANES))], [struct(GOT_X, BF16), struct((64, LANES), jnp.int32)],
        [STATE, MASK, STATE, pltpu.VMEM((8, LANES), F32)], 4,
    )(z, g, d, b, u)


def local_x(g, d, b, c, u):
    return call(
        local_x_kernel, "local_x", STEPS,
        [fixed(FLAT), fixed(FLAT), block(ROW, each), block(ROW, each), block(ROW, each)],
        [block(ROW, each), block(ROW, each), fixed(FLAT)],
        [struct((TOK, LANES), F32), struct((TOK, LANES), F32), struct(FLAT, F32)],
        [STATE, STATE, pltpu.VMEM(ENDS, F32), MASK, STATE], 12,
    )(g, d, b, c, u)


def send_x(y, c, back, e, got):
    return call(
        send_x_kernel, "send_x", 2 * STEPS,
        [block(ROW, early), block(ROW, early), block(ROW, early), fixed(FLAT), fixed(GOT_X)],
        block(ROW, late), struct((TOK, LANES), BF16),
        [
            STATE, pltpu.VMEM((TOK, LANES), F32),
            pltpu.VMEM((64, LANES), jnp.int32), pltpu.SMEM((64, LANES), jnp.int32), pltpu.SemaphoreType.DMA,
        ], 12, loose=4,
    )(y, c, back, e, got)


def before_z(g, d, b, c, gate):
    return call(
        before_z_kernel, "before_z", STEPS,
        [fixed(FLAT), fixed(FLAT), block(ROW, each), block(ROW, each), block(ROW, each)],
        [
            block(ROW, each), block((CHUNK, STEP), lambda i: (0, i)), block(ROW, each), block(ROW, each),
            fixed((8, LANES)), fixed(FLAT), fixed(FLAT), fixed(ENDS),
        ],
        [
            struct((TOK, LANES), BF16), struct((CHUNK, TOK), BF16), struct((TOK, LANES), F32),
            struct((TOK, LANES), F32), struct((8, LANES), F32), struct(FLAT, F32), struct(FLAT, F32),
            struct(ENDS, F32),
        ],
        [STATE, STATE, MASK], 18,
    )(g, d, b, c, gate)


def states_z(place, t, f, scale, b_t, got):
    return call(
        states_z_kernel, "states_z", 2 * STEPS,
        [
            fixed((8, LANES)), fixed(FLAT), block(ROW, late),
            block((CHUNK, STEP), lambda i, _: (0, jnp.maximum(i - STEPS, 0))), block(ROW, early),
        ],
        [block(ROW, late), fixed(GOT_Z)],
        [struct((TOK, LANES), BF16), struct(GOT_Z, BF16)],
        [STATE, pltpu.VMEM((TOK, LANES), F32)], 10, prefetch=1, loose=5,
    )(place, t, f, scale, b_t, got)


def local_z(u2, s, b_t, c, back, ends):
    return call(
        local_z_kernel, "local_z", STEPS,
        [
            block(ROW, each), block(ROW, each), block((CHUNK, STEP), lambda i: (0, i)), block(ROW, each),
            block(ROW, each), fixed(ENDS),
        ],
        block(ROW, each), struct((TOK, LANES), F32), [STATE], 14,
    )(u2, s, b_t, c, back, ends)


def gate_z(y, c, back, e, got):
    return call(
        gate_z_kernel, "gate_z", STEPS,
        [block(ROW, each), block(ROW, each), block(ROW, each), fixed(FLAT), fixed(GOT_Z)],
        block(ROW, each), struct((TOK, LANES), BF16), [STATE], 12, loose=4,
    )(y, c, back, e, got)


def final(x, w):
    rows = 1024
    return call(
        final_kernel, "final", 1024 // rows,
        [block((8, rows, LANES), lambda i: (0, i, 0)), fixed((8, WROWS, 512))],
        block((rows, 512), each), struct((1024, 512), BF16), [], 5, limit=20, loose=0,
    )(x, w)


def three_pieces(value):
    high = lax.reduce_precision(value, 8, 7)
    mid = lax.reduce_precision(value - high, 8, 7)
    return high, mid, value - high - mid


def flat(value):
    return value.reshape(2, TOK // CHUNK, CHUNK).transpose(1, 0, 2).reshape(CHUNK, LANES)


def body(
    x_inputs,
    x_in_proj,
    x_out_proj,
    x_log_decay,
    x_step,
    z_source,
    z_in_proj,
    z_out_proj,
    z_log_decay,
    z_step,
    gate_branch,
    norm_gain,
    out_weight,
):
    g_x, d_x = flat(x_log_decay), flat(x_step)
    message, place = states_x(z_source.reshape(64, LANES), g_x, d_x, x_in_proj, x_inputs)
    message, g_x, d_x = lax.optimization_barrier((message, g_x, d_x))
    got_x = lax.all_to_all(message, "seq", 0, 0)
    y_x, back_x, e_x = local_x(g_x, d_x, x_in_proj, x_out_proj, x_inputs)
    sent = send_x(y_x, x_out_proj, back_x, e_x, got_x)
    sent, g_z, d_z, norm_gain, out_weight = lax.optimization_barrier(
        (sent, z_log_decay, z_step, norm_gain, out_weight)
    )
    gain = jnp.pad(jnp.stack(three_pieces(norm_gain)), ((0, WROWS - LANES - 3), (0, 512 - LANES))).astype(BF16)
    weights = lax.all_gather(jnp.concatenate([out_weight, gain], axis=0), "head", axis=0, tiled=False)
    received = lax.all_to_all(sent.reshape(GROUPS, PIECE, LANES), "seq", 0, 0).reshape(TOK, LANES)
    s_z, b_t, scale_z, back_z, t_z, f_z, e_z, ends_z = before_z(
        flat(g_z), flat(d_z), z_in_proj, z_out_proj, gate_branch
    )
    received, weights = lax.optimization_barrier((received, weights))
    u2_z, tails_z = states_z(place, t_z, f_z, scale_z, b_t, received)
    got_z = lax.all_to_all(tails_z, "seq", 0, 0)
    y_z = local_z(u2_z, s_z, b_t, z_out_proj, back_z, ends_z)
    gated = gate_z(y_z, z_out_proj, back_z, e_z, got_z)
    whole = lax.all_to_all(gated.reshape(8, 1024, LANES), "head", 0, 0)
    return final(whole, weights)


def solution(mesh):
    placed = (
        P("seq", "head"),
        P("seq", None),
        P("seq", None),
        P("head", "seq"),
        P("head", "seq"),
        P("seq"),
        P("seq", None),
        P("seq", None),
        P("head", "seq"),
        P("head", "seq"),
        P("seq", "head"),
        P("head"),
        P("head", None),
    )
    return jax.shard_map(
        body, mesh=mesh, in_specs=placed, out_specs=P(("seq", "head"), None), check_vma=False
    )
```

```python
import math

import jax
import jax.numpy as jnp
from jax import lax
from jax.experimental import pallas as pl
from jax.experimental.pallas import tpu as pltpu
from jax.sharding import PartitionSpec as P

TOK = 8192
LANES = 128
CHUNK = 128
STEP = 4096
PER = STEP // CHUNK
STEPS = TOK // STEP
PIECE = 512
GROUPS = 16
TAIL = 144
MSG = 160
WROWS = 136
TOGETHER = 32
LINES = 2
F32 = jnp.float32
BF16 = jnp.bfloat16


def mm(a, b):
    return jnp.dot(a, b, preferred_element_type=F32)


def nt(a, b):
    return lax.dot_general(a, b, (((1,), (1,)), ((), ())), preferred_element_type=F32)


def tn(a, b):
    return lax.dot_general(a, b, (((0,), (0,)), ((), ())), preferred_element_type=F32)


def iotas():
    shape = (CHUNK, CHUNK)
    return lax.broadcasted_iota(jnp.int32, shape, 0), lax.broadcasted_iota(jnp.int32, shape, 1)


def ones(condition):
    return jnp.where(condition, 1.0, 0.0).astype(BF16)


def pieces(value, axis):
    high = value.astype(BF16)
    rest = value - high.astype(F32)
    mid = rest.astype(BF16)
    low = (rest - mid.astype(F32)).astype(BF16)
    return jnp.concatenate([high, mid, low], axis=axis)


def thrice(mask, axis):
    return jnp.concatenate([mask, mask, mask], axis=axis)


def wide(column):
    return jnp.broadcast_to(column, (CHUNK, LANES))


def by_head(first, second):
    return jnp.where(lax.broadcasted_iota(jnp.int32, (1, LANES), 1) < 64, first, second)


def row_pair(slab, at):
    return by_head(slab[2 * at : 2 * at + 1], slab[2 * at + 1 : 2 * at + 2])


def spread_mask():
    row = lax.broadcasted_iota(jnp.int32, (6 * PER, STEP), 0) & (2 * PER - 1)
    col = lax.broadcasted_iota(jnp.int32, (6 * PER, STEP), 1)
    return ones(row == 2 * (col >> 7) + ((col >> 6) & 1))


def spread(slab, mask):
    return tn(pieces(slab, 0), mask)


def slab_at(step):
    return pl.ds(pl.multiple_of(2 * PER * step, 2 * PER), 2 * PER)


def end_weights(g, d):
    row, col = iotas()
    inner = mm(pieces(g, 1), thrice(ones(row > col), 0))
    total = wide(inner[:, 0:1] + g[:, 0:1])
    later = mm(thrice(ones((col > row) & ((col & 1) == (row & 1))), 1), pieces(total, 0))
    whole = later[0:2] + total[0:2]
    return jnp.exp(inner + later) * d, by_head(whole[0:1], whole[1:2])


def scan_factors(g, d):
    row, col = iotas()
    cum = mm(pieces(g, 1), thrice(ones(row <= col), 0))
    mid = wide(cum[:, CHUNK // 2 - 1 : CHUNK // 2])
    total = wide(cum[:, CHUNK - 1 : CHUNK])
    same = (col & 1) == (row & 1)
    before = mm(thrice(ones((col < row) & same), 1), pieces(total, 0))
    after = mm(thrice(ones((col > row) & same), 1), pieces(total, 0))
    return (
        jnp.exp(mid - cum) * d,
        jnp.exp(cum - mid),
        jnp.exp(mid),
        jnp.exp(total),
        jnp.exp(total - mid),
        jnp.exp(mid + before),
        jnp.exp(total - mid + after),
    )


def write_tail(msg_ref, state, total):
    high = total.astype(BF16).astype(F32)
    mid = (total - high).astype(BF16).astype(F32)
    low = total - high - mid
    pad = jnp.zeros((TAIL - CHUNK - 3, LANES), F32)
    tail = jnp.concatenate([state, high, mid, low, pad], axis=0).astype(BF16)
    for k in range(GROUPS):
        msg_ref[k, 0:TAIL, :] = tail


def match_rows(index, count):
    return lax.broadcasted_iota(jnp.int32, (count, LANES), 0) == index


def route(z_ref, msg_ref, place_ref):
    z = z_ref[...]
    group, token = z >> 13, z & (TOK - 1)
    row, col = iotas()
    hits = [group == k for k in range(GROUPS)]
    inside = mm(jnp.concatenate([ones(hit) for hit in hits], axis=0), ones(row <= col))
    counts = [inside[64 * k : 64 * k + 64] for k in range(GROUPS)]
    sums = jnp.concatenate([jnp.broadcast_to(count[:, 127:128], (64, LANES)) for count in counts], axis=1)
    above = mm(ones(row > col)[0:64, 0:64], sums.astype(BF16))
    slot = jnp.zeros((64, LANES), F32)
    for k in range(GROUPS):
        rank = counts[k] + above[:, k * LANES : (k + 1) * LANES] + float(k * PIECE - 1)
        slot = jnp.where(hits[k], rank, slot)
    slot = slot.astype(jnp.int32)
    place_ref[...] = slot
    slot_high, slot_low = slot >> 7, slot & 127
    token_high, token_low = (token >> 7).astype(F32), (token & 127).astype(F32)
    total = jnp.zeros((LANES, LANES), F32)
    for base in range(0, 64, 4):
        lefts, rights = [], []
        for q in range(base, base + 4):
            hit = match_rows(slot_high[q : q + 1], 64)
            values = (token_high[q : q + 1], token_low[q : q + 1])
            lefts.append(jnp.concatenate([jnp.where(hit, value, 0.0) for value in values], axis=0).astype(BF16))
            rights.append(ones(match_rows(slot_low[q : q + 1], LANES)))
        total = total + nt(jnp.concatenate(lefts, axis=1), jnp.concatenate(rights, axis=1))
    for k in range(GROUPS):
        rows = slice(4 * k, 4 * k + 4)
        wanted = jnp.concatenate([total[rows], total[64 + 4 * k : 68 + 4 * k], jnp.zeros((8, LANES), F32)], axis=0)
        msg_ref[k, TAIL:MSG, :] = wanted.astype(BF16)


def chunk_rows(at):
    return slice(at * CHUNK, (at + 1) * CHUNK)


def states_x_kernel(z_ref, g_ref, d_ref, b_ref, u_ref, msg_ref, place_ref, weights, mask, state, total):
    step = pl.program_id(0)

    @pl.when(step == 0)
    def _():
        route(z_ref, msg_ref, place_ref)
        weights[...], total[0:1, :] = end_weights(g_ref[...], d_ref[...])
        mask[...] = spread_mask()
        state[...] = jnp.zeros_like(state)

    scale = spread(weights[slab_at(step), :], mask[...])
    parts = [
        (u_ref[chunk_rows(at), :].astype(F32) * scale[:, chunk_rows(at)]).astype(BF16) for at in range(PER)
    ]
    state[...] += tn(b_ref[...], jnp.concatenate(parts, axis=0))

    @pl.when(step == STEPS - 1)
    def _():
        write_tail(msg_ref, state[...], total[0:1, :])


def local_scan(u2s, scores, b_ts, cs, slabs, state, finish):
    into, end, add = slabs
    carry = state[...]
    sums = [mm(b_ts[at], u2s[at]) for at in range(PER)]
    helds = []
    for at in range(PER):
        helds.append((carry * row_pair(into, at)).astype(BF16))
        carry = row_pair(end, at) * carry + row_pair(add, at) * sums[at]
    state[...] = carry
    for at in range(PER):
        left = jnp.concatenate([scores[at], cs[at]], axis=1)
        right = jnp.concatenate([u2s[at], helds[at]], axis=0)
        finish(at, mm(left, right))


def local_x_kernel(g_ref, d_ref, b_ref, c_ref, u_ref, y_ref, back_ref, e_ref, a_all, r_all, ends, mask, state):
    step = pl.program_id(0)

    @pl.when(step == 0)
    def _():
        a_all[...], r_all[...], ends[0], ends[1], ends[2], e_ref[...], _ = scan_factors(g_ref[...], d_ref[...])
        mask[...] = spread_mask()
        state[...] = jnp.zeros_like(state)

    row, col = iotas()
    lower = row >= col
    here = slab_at(step)
    scale = spread(a_all[here, :], mask[...])
    u2s = [(u_ref[chunk_rows(at), :].astype(F32) * scale[:, chunk_rows(at)]).astype(BF16) for at in range(PER)]
    b_ts = [b_ref[chunk_rows(at), :].T for at in range(PER)]
    cs = [c_ref[chunk_rows(at), :] for at in range(PER)]
    scores = [jnp.where(lower, mm(cs[at], b_ts[at]), 0.0).astype(BF16) for at in range(PER)]
    slabs = (ends[0, here, :], ends[1, here, :], ends[2, here, :])

    back = spread(r_all[here, :], mask[...])

    def finish(at, value):
        y_ref[chunk_rows(at), :] = (back[:, chunk_rows(at)] * value).astype(BF16)
        back_ref[chunk_rows(at), :] = back[:, chunk_rows(at)]

    local_scan(u2s, scores, b_ts, cs, slabs, state, finish)


def start_state(got_ref, state):
    me = lax.axis_index("seq")
    state[...] = jnp.zeros_like(state)
    for k in range(GROUPS - 1):

        @pl.when(k < me)
        def _():
            tail = got_ref[k, CHUNK:TAIL, :].astype(F32)
            decay = jnp.exp(tail[0:1] + tail[1:2] + tail[2:3])
            state[...] = decay * state[...] + got_ref[k, 0:CHUNK, :].astype(F32)


def add_start(y_ref, c_ref, back_ref, e_slab, state, out_ref, base=0):
    start = state[...]
    for at in range(PER):
        rows = chunk_rows(at)
        held = (start * row_pair(e_slab, at)).astype(BF16)
        value = y_ref[rows, :].astype(F32) + back_ref[rows, :] * mm(c_ref[rows, :], held)
        out_ref[pl.ds(pl.multiple_of(base + at * CHUNK, CHUNK), CHUNK), :] = value.astype(out_ref.dtype)


def read_lists(got_ref, slots):
    for k in range(GROUPS):
        lists = got_ref[k, TAIL:MSG, :].astype(F32)
        slots[4 * k : 4 * k + 4, :] = (lists[0:4] * 128.0 + lists[4:8]).astype(jnp.int32)


def take_rows(source, table, line, first, count):
    return jnp.concatenate([source[pl.ds(table[line, first + k], 1), :] for k in range(count)], axis=0)


def send_x_kernel(
    y_ref, c_ref, back_ref, e_ref, got_ref, out_ref, state, rows, slots, table, sem
):
    step = pl.program_id(0)

    @pl.when(step == 0)
    def _():
        read_lists(got_ref, slots)
        pltpu.make_async_copy(slots, table, sem).start()
        start_state(got_ref, state)

    @pl.when(step < STEPS)
    def _():
        base = step * STEP
        add_start(y_ref, c_ref, back_ref, e_ref[slab_at(step), :], state, rows, base)

    @pl.when(step == 0)
    def _():
        pltpu.make_async_copy(slots, table, sem).wait()

    @pl.when(step >= STEPS)
    def _():
        def take(i, _):
            for at in range(LINES):
                line = i * LINES + at
                for q in range(LANES // 16):
                    here = pl.ds(pl.multiple_of(line * LANES + q * 16, 16), 16)
                    out_ref[here, :] = take_rows(rows, table, (step - STEPS) * PER + line, q * 16, 16).astype(BF16)
            return 0

        lax.fori_loop(0, PER // LINES, take, 0)


def before_z_kernel(
    g_ref, d_ref, b_ref, c_ref, gate_ref,
    s_ref, b_t_ref, scale_ref, back_ref, t_ref, f_ref, e_ref, ends_ref, a_all, r_all, mask,
):
    step = pl.program_id(0)

    @pl.when(step == 0)
    def _():
        _, total = end_weights(g_ref[...], d_ref[...])
        t_ref[...] = jnp.broadcast_to(total, (8, LANES))
        a_all[...], r_all[...], ends_ref[0], ends_ref[1], ends_ref[2], e_ref[...], f_ref[...] = scan_factors(
            g_ref[...], d_ref[...]
        )
        mask[...] = spread_mask()

    row, col = iotas()
    lower = row >= col
    here = slab_at(step)
    scale = spread(a_all[here, :], mask[...])
    back = spread(r_all[here, :], mask[...])
    for at in range(PER):
        rows = chunk_rows(at)
        b_t = b_ref[rows, :].T
        b_t_ref[:, rows] = b_t
        s_ref[rows, :] = jnp.where(lower, mm(c_ref[rows, :], b_t), 0.0).astype(BF16)
        scale_ref[rows, :] = scale[:, rows]
        gate = gate_ref[rows, :].astype(F32)
        silu = gate * (0.5 * jnp.tanh(0.5 * gate) + 0.5)
        back_ref[rows, :] = silu * back[:, rows]


def states_z_kernel(
    place_ref, t_ref, f_ref, scale_ref, b_t_ref, got_ref, u2_ref, msg_ref, state, rows, place, sem
):
    step = pl.program_id(0)

    @pl.when(step == 0)
    def _():
        pltpu.make_async_copy(place_ref, place, sem).start()
        state[...] = jnp.zeros_like(state)

    @pl.when(step < STEPS)
    def _():
        rows[pl.ds(pl.multiple_of(step * STEP, STEP), STEP), :] = got_ref[...].astype(F32)

    @pl.when(step == 0)
    def _():
        pltpu.make_async_copy(place_ref, place, sem).wait()

    @pl.when(step >= STEPS)
    def _():
        block_at = step - STEPS

        def one(i, total):
            for at in range(TOGETHER):
                chunk = i * TOGETHER + at
                here = pl.ds(pl.multiple_of(chunk * CHUNK, CHUNK), CHUNK)
                line = block_at * PER + chunk
                u = take_rows(rows, place, line, 0, CHUNK)
                u2 = (u * scale_ref[here, :]).astype(BF16)
                u2_ref[here, :] = u2
                factor = by_head(f_ref[pl.ds(2 * line, 1), :], f_ref[pl.ds(2 * line + 1, 1), :])
                total = total + factor * mm(b_t_ref[:, here], u2)
            return total

        state[...] = lax.fori_loop(0, PER // TOGETHER, one, state[...])

    @pl.when(step == 2 * STEPS - 1)
    def _():
        write_tail(msg_ref, state[...], t_ref[0:1, :])


def local_z_kernel(u2_ref, s_ref, b_t_ref, c_ref, back_ref, ends_ref, y_ref, state):
    step = pl.program_id(0)

    @pl.when(step == 0)
    def _():
        state[...] = jnp.zeros_like(state)

    here = slab_at(step)
    u2s = [u2_ref[chunk_rows(at), :] for at in range(PER)]
    scores = [s_ref[chunk_rows(at), :] for at in range(PER)]
    b_ts = [b_t_ref[:, chunk_rows(at)] for at in range(PER)]
    cs = [c_ref[chunk_rows(at), :] for at in range(PER)]
    slabs = (ends_ref[0, here, :], ends_ref[1, here, :], ends_ref[2, here, :])

    def finish(at, value):
        y_ref[chunk_rows(at), :] = (back_ref[chunk_rows(at), :] * value).astype(BF16)

    local_scan(u2s, scores, b_ts, cs, slabs, state, finish)


def gate_z_kernel(y_ref, c_ref, back_ref, e_ref, got_ref, out_ref, state):
    step = pl.program_id(0)

    @pl.when(step == 0)
    def _():
        start_state(got_ref, state)

    add_start(y_ref, c_ref, back_ref, e_ref[slab_at(step), :], state, out_ref)


def final_kernel(x_ref, w_ref, out_ref):
    parts = [x_ref[k].astype(F32) for k in range(8)]
    squares = sum(part * part for part in parts)
    mean = jnp.sum(squares, axis=1, keepdims=True) * (1.0 / 1024.0)
    scale = lax.rsqrt(mean + 1e-05)
    total = None
    for k in range(8):
        parts3 = w_ref[k, LANES:WROWS, 0:LANES].astype(F32)
        gain = parts3[0:1] + parts3[1:2] + parts3[2:3]
        term = mm((parts[k] * scale * gain).astype(BF16), w_ref[k, 0:LANES, :])
        total = term if total is None else total + term
    out_ref[...] = total.astype(BF16)


ROW = (STEP, LANES)
FLAT = (CHUNK, LANES)
GOT_X = (GROUPS, MSG, LANES)
GOT_Z = (GROUPS, TAIL, LANES)
ENDS = (3, CHUNK, LANES)
MASK = pltpu.VMEM((6 * PER, STEP), BF16)
STATE = pltpu.VMEM(FLAT, F32)


def block(shape, index):
    return pl.BlockSpec(shape, index)


def fixed(shape):
    return pl.BlockSpec(shape, lambda *_: (0,) * len(shape))


def each(i, *_):
    return (i, 0)


def early(i, *_):
    return (jnp.minimum(i, STEPS - 1), 0)


def late(i, *_):
    return (jnp.maximum(i - STEPS, 0), 0)


def struct(shape, dtype):
    return jax.ShapeDtypeStruct(shape, dtype)


def call(kernel, name, steps, ins, outs, shapes, scratch, mib, prefetch=0, limit=36, loose=-1):
    large = 1 << 13
    shapes = jax.tree.map(
        lambda shape: pltpu.HBM(shape.shape, shape.dtype) if math.prod(shape.shape) >= large else shape, shapes
    )
    made = pl.pallas_call(
        kernel,
        name=name,
        grid_spec=pltpu.PrefetchScalarGridSpec(
            num_scalar_prefetch=prefetch, grid=(steps,), in_specs=ins, out_specs=outs, scratch_shapes=scratch
        ),
        out_shape=shapes,
        compiler_params=pltpu.CompilerParams(
            dimension_semantics=("arbitrary",), vmem_limit_bytes=limit * 1024 * 1024
        ),
        cost_estimate=pl.CostEstimate(flops=mib << 28, bytes_accessed=mib << 20, transcendentals=0),
    )

    def run(*values):
        return made(
            *[
                pltpu.with_memory_space_constraint(value, pltpu.HBM)
                if at != loose and value.size >= large
                else value
                for at, value in enumerate(values)
            ]
        )

    return run


def states_x(z, g, d, b, u):
    return call(
        states_x_kernel, "states_x", STEPS,
        [fixed((64, LANES)), fixed(FLAT), fixed(FLAT), block(ROW, each), block(ROW, each)],
        [fixed(GOT_X), fixed((64, LANES))], [struct(GOT_X, BF16), struct((64, LANES), jnp.int32)],
        [STATE, MASK, STATE, pltpu.VMEM((8, LANES), F32)], 4,
    )(z, g, d, b, u)


def local_x(g, d, b, c, u):
    return call(
        local_x_kernel, "local_x", STEPS,
        [fixed(FLAT), fixed(FLAT), block(ROW, each), block(ROW, each), block(ROW, each)],
        [block(ROW, each), block(ROW, each), fixed(FLAT)],
        [struct((TOK, LANES), BF16), struct((TOK, LANES), F32), struct(FLAT, F32)],
        [STATE, STATE, pltpu.VMEM(ENDS, F32), MASK, STATE], 12,
    )(g, d, b, c, u)


def send_x(y, c, back, e, got):
    return call(
        send_x_kernel, "send_x", 2 * STEPS,
        [block(ROW, early), block(ROW, early), block(ROW, early), fixed(FLAT), fixed(GOT_X)],
        block(ROW, late), struct((TOK, LANES), BF16),
        [
            STATE, pltpu.VMEM((TOK, LANES), F32),
            pltpu.VMEM((64, LANES), jnp.int32), pltpu.SMEM((64, LANES), jnp.int32), pltpu.SemaphoreType.DMA,
        ], 12, loose=4,
    )(y, c, back, e, got)


def before_z(g, d, b, c, gate):
    return call(
        before_z_kernel, "before_z", STEPS,
        [fixed(FLAT), fixed(FLAT), block(ROW, each), block(ROW, each), block(ROW, each)],
        [
            block(ROW, each), block((CHUNK, STEP), lambda i: (0, i)), block(ROW, each), block(ROW, each),
            fixed((8, LANES)), fixed(FLAT), fixed(FLAT), fixed(ENDS),
        ],
        [
            struct((TOK, LANES), BF16), struct((CHUNK, TOK), BF16), struct((TOK, LANES), F32),
            struct((TOK, LANES), F32), struct((8, LANES), F32), struct(FLAT, F32), struct(FLAT, F32),
            struct(ENDS, F32),
        ],
        [STATE, STATE, MASK], 18,
    )(g, d, b, c, gate)


def states_z(place, t, f, scale, b_t, got):
    return call(
        states_z_kernel, "states_z", 2 * STEPS,
        [
            fixed((64, LANES)), fixed((8, LANES)), fixed(FLAT), block(ROW, late),
            block((CHUNK, STEP), lambda i: (0, jnp.maximum(i - STEPS, 0))), block(ROW, early),
        ],
        [block(ROW, late), fixed(GOT_Z)],
        [struct((TOK, LANES), BF16), struct(GOT_Z, BF16)],
        [
            STATE, pltpu.VMEM((TOK, LANES), F32), pltpu.SMEM((64, LANES), jnp.int32), pltpu.SemaphoreType.DMA,
        ], 10, loose=5,
    )(place, t, f, scale, b_t, got)


def local_z(u2, s, b_t, c, back, ends):
    return call(
        local_z_kernel, "local_z", STEPS,
        [
            block(ROW, each), block(ROW, each), block((CHUNK, STEP), lambda i: (0, i)), block(ROW, each),
            block(ROW, each), fixed(ENDS),
        ],
        block(ROW, each), struct((TOK, LANES), BF16), [STATE], 14,
    )(u2, s, b_t, c, back, ends)


def gate_z(y, c, back, e, got):
    return call(
        gate_z_kernel, "gate_z", STEPS,
        [block(ROW, each), block(ROW, each), block(ROW, each), fixed(FLAT), fixed(GOT_Z)],
        block(ROW, each), struct((TOK, LANES), BF16), [STATE], 12, loose=4,
    )(y, c, back, e, got)


def final(x, w):
    rows = 1024
    return call(
        final_kernel, "final", 1024 // rows,
        [block((8, rows, LANES), lambda i: (0, i, 0)), fixed((8, WROWS, 512))],
        block((rows, 512), each), struct((1024, 512), BF16), [], 5, limit=20, loose=0,
    )(x, w)


def three_pieces(value):
    high = lax.reduce_precision(value, 8, 7)
    mid = lax.reduce_precision(value - high, 8, 7)
    return high, mid, value - high - mid


def flat(value):
    return value.reshape(2, TOK // CHUNK, CHUNK).transpose(1, 0, 2).reshape(CHUNK, LANES)


def body(
    x_inputs,
    x_in_proj,
    x_out_proj,
    x_log_decay,
    x_step,
    z_source,
    z_in_proj,
    z_out_proj,
    z_log_decay,
    z_step,
    gate_branch,
    norm_gain,
    out_weight,
):
    g_x, d_x = flat(x_log_decay), flat(x_step)
    message, place = states_x(z_source.reshape(64, LANES), g_x, d_x, x_in_proj, x_inputs)
    message, g_x, d_x = lax.optimization_barrier((message, g_x, d_x))
    got_x = lax.all_to_all(message, "seq", 0, 0)
    y_x, back_x, e_x = local_x(g_x, d_x, x_in_proj, x_out_proj, x_inputs)
    sent = send_x(y_x, x_out_proj, back_x, e_x, got_x)
    sent, g_z, d_z, norm_gain, out_weight = lax.optimization_barrier(
        (sent, z_log_decay, z_step, norm_gain, out_weight)
    )
    gain = jnp.pad(jnp.stack(three_pieces(norm_gain)), ((0, WROWS - LANES - 3), (0, 512 - LANES))).astype(BF16)
    weights = lax.all_gather(jnp.concatenate([out_weight, gain], axis=0), "head", axis=0, tiled=False)
    received = lax.all_to_all(sent.reshape(GROUPS, PIECE, LANES), "seq", 0, 0).reshape(TOK, LANES)
    s_z, b_t, scale_z, back_z, t_z, f_z, e_z, ends_z = before_z(
        flat(g_z), flat(d_z), z_in_proj, z_out_proj, gate_branch
    )
    received, weights = lax.optimization_barrier((received, weights))
    u2_z, tails_z = states_z(place, t_z, f_z, scale_z, b_t, received)
    got_z = lax.all_to_all(tails_z, "seq", 0, 0)
    y_z = local_z(u2_z, s_z, b_t, z_out_proj, back_z, ends_z)
    gated = gate_z(y_z, z_out_proj, back_z, e_z, got_z)
    whole = lax.all_to_all(gated.reshape(8, 1024, LANES), "head", 0, 0)
    return final(whole, weights)


def solution(mesh):
    placed = (
        P("seq", "head"),
        P("seq", None),
        P("seq", None),
        P("head", "seq"),
        P("head", "seq"),
        P("seq"),
        P("seq", None),
        P("seq", None),
        P("head", "seq"),
        P("head", "seq"),
        P("seq", "head"),
        P("head"),
        P("head", None),
    )
    return jax.shard_map(
        body, mesh=mesh, in_specs=placed, out_specs=P(("seq", "head"), None), check_vma=False
    )
```

```python
import math

import jax
import jax.numpy as jnp
from jax import lax
from jax.experimental import pallas as pl
from jax.experimental.pallas import tpu as pltpu
from jax.sharding import PartitionSpec as P

TOK = 8192
LANES = 128
CHUNK = 128
STEP = 4096
PER = STEP // CHUNK
STEPS = TOK // STEP
PIECE = 512
GROUPS = 16
TAIL = 144
MSG = 160
WROWS = 136
TOGETHER = 32
LINES = 2
F32 = jnp.float32
BF16 = jnp.bfloat16


def mm(a, b):
    return jnp.dot(a, b, preferred_element_type=F32)


def nt(a, b):
    return lax.dot_general(a, b, (((1,), (1,)), ((), ())), preferred_element_type=F32)


def tn(a, b):
    return lax.dot_general(a, b, (((0,), (0,)), ((), ())), preferred_element_type=F32)


def iotas():
    shape = (CHUNK, CHUNK)
    return lax.broadcasted_iota(jnp.int32, shape, 0), lax.broadcasted_iota(jnp.int32, shape, 1)


def ones(condition):
    return jnp.where(condition, 1.0, 0.0).astype(BF16)


def pieces(value, axis):
    high = value.astype(BF16)
    rest = value - high.astype(F32)
    mid = rest.astype(BF16)
    low = (rest - mid.astype(F32)).astype(BF16)
    return jnp.concatenate([high, mid, low], axis=axis)


def thrice(mask, axis):
    return jnp.concatenate([mask, mask, mask], axis=axis)


def wide(column):
    return jnp.broadcast_to(column, (CHUNK, LANES))


def by_head(first, second):
    return jnp.where(lax.broadcasted_iota(jnp.int32, (1, LANES), 1) < 64, first, second)


def row_pair(slab, at):
    return by_head(slab[2 * at : 2 * at + 1], slab[2 * at + 1 : 2 * at + 2])


def spread_mask():
    row = lax.broadcasted_iota(jnp.int32, (6 * PER, STEP), 0) & (2 * PER - 1)
    col = lax.broadcasted_iota(jnp.int32, (6 * PER, STEP), 1)
    return ones(row == 2 * (col >> 7) + ((col >> 6) & 1))


def spread(slab, mask):
    return tn(pieces(slab, 0), mask)


def slab_at(step):
    return pl.ds(pl.multiple_of(2 * PER * step, 2 * PER), 2 * PER)


def end_weights(g, d):
    row, col = iotas()
    inner = mm(pieces(g, 1), thrice(ones(row > col), 0))
    total = wide(inner[:, 0:1] + g[:, 0:1])
    later = mm(thrice(ones((col > row) & ((col & 1) == (row & 1))), 1), pieces(total, 0))
    whole = later[0:2] + total[0:2]
    return jnp.exp(inner + later) * d, by_head(whole[0:1], whole[1:2])


def scan_factors(g, d):
    row, col = iotas()
    cum = mm(pieces(g, 1), thrice(ones(row <= col), 0))
    mid = wide(cum[:, CHUNK // 2 - 1 : CHUNK // 2])
    total = wide(cum[:, CHUNK - 1 : CHUNK])
    same = (col & 1) == (row & 1)
    before = mm(thrice(ones((col < row) & same), 1), pieces(total, 0))
    after = mm(thrice(ones((col > row) & same), 1), pieces(total, 0))
    return (
        jnp.exp(mid - cum) * d,
        jnp.exp(cum - mid),
        jnp.exp(mid),
        jnp.exp(total),
        jnp.exp(total - mid),
        jnp.exp(mid + before),
        jnp.exp(total - mid + after),
    )


def write_tail(msg_ref, state, total):
    high = total.astype(BF16).astype(F32)
    mid = (total - high).astype(BF16).astype(F32)
    low = total - high - mid
    pad = jnp.zeros((TAIL - CHUNK - 3, LANES), F32)
    tail = jnp.concatenate([state, high, mid, low, pad], axis=0).astype(BF16)
    for k in range(GROUPS):
        msg_ref[k, 0:TAIL, :] = tail


def match_rows(index, count):
    return lax.broadcasted_iota(jnp.int32, (count, LANES), 0) == index


def route(z_ref, msg_ref, place_ref):
    z = z_ref[...]
    group, token = z >> 13, z & (TOK - 1)
    row, col = iotas()
    hits = [group == k for k in range(GROUPS)]
    inside = mm(jnp.concatenate([ones(hit) for hit in hits], axis=0), ones(row <= col))
    counts = [inside[64 * k : 64 * k + 64] for k in range(GROUPS)]
    sums = jnp.concatenate([jnp.broadcast_to(count[:, 127:128], (64, LANES)) for count in counts], axis=1)
    above = mm(ones(row > col)[0:64, 0:64], sums.astype(BF16))
    slot = jnp.zeros((64, LANES), F32)
    for k in range(GROUPS):
        rank = counts[k] + above[:, k * LANES : (k + 1) * LANES] + float(k * PIECE - 1)
        slot = jnp.where(hits[k], rank, slot)
    slot = slot.astype(jnp.int32)
    place_ref[...] = slot
    slot_high, slot_low = slot >> 7, slot & 127
    token_high, token_low = (token >> 7).astype(F32), (token & 127).astype(F32)
    total = jnp.zeros((LANES, LANES), F32)
    for base in range(0, 64, 4):
        lefts, rights = [], []
        for q in range(base, base + 4):
            hit = match_rows(slot_high[q : q + 1], 64)
            values = (token_high[q : q + 1], token_low[q : q + 1])
            lefts.append(jnp.concatenate([jnp.where(hit, value, 0.0) for value in values], axis=0).astype(BF16))
            rights.append(ones(match_rows(slot_low[q : q + 1], LANES)))
        total = total + nt(jnp.concatenate(lefts, axis=1), jnp.concatenate(rights, axis=1))
    for k in range(GROUPS):
        rows = slice(4 * k, 4 * k + 4)
        wanted = jnp.concatenate([total[rows], total[64 + 4 * k : 68 + 4 * k], jnp.zeros((8, LANES), F32)], axis=0)
        msg_ref[k, TAIL:MSG, :] = wanted.astype(BF16)


def chunk_rows(at):
    return slice(at * CHUNK, (at + 1) * CHUNK)


def states_x_kernel(z_ref, g_ref, d_ref, b_ref, u_ref, msg_ref, place_ref, weights, mask, state, total):
    step = pl.program_id(0)

    @pl.when(step == 0)
    def _():
        route(z_ref, msg_ref, place_ref)
        weights[...], total[0:1, :] = end_weights(g_ref[...], d_ref[...])
        mask[...] = spread_mask()
        state[...] = jnp.zeros_like(state)

    scale = spread(weights[slab_at(step), :], mask[...])
    parts = [
        (u_ref[chunk_rows(at), :].astype(F32) * scale[:, chunk_rows(at)]).astype(BF16) for at in range(PER)
    ]
    state[...] += tn(b_ref[...], jnp.concatenate(parts, axis=0))

    @pl.when(step == STEPS - 1)
    def _():
        write_tail(msg_ref, state[...], total[0:1, :])


def local_scan(u2s, scores, b_ts, cs, slabs, state, finish):
    into, end, add = slabs
    carry = state[...]
    sums = [mm(b_ts[at], u2s[at]) for at in range(PER)]
    helds = []
    for at in range(PER):
        helds.append((carry * row_pair(into, at)).astype(BF16))
        carry = row_pair(end, at) * carry + row_pair(add, at) * sums[at]
    state[...] = carry
    for at in range(PER):
        left = jnp.concatenate([scores[at], cs[at]], axis=1)
        right = jnp.concatenate([u2s[at], helds[at]], axis=0)
        finish(at, mm(left, right))


def local_x_kernel(g_ref, d_ref, b_ref, c_ref, u_ref, y_ref, back_ref, e_ref, a_all, r_all, ends, mask, state):
    step = pl.program_id(0)

    @pl.when(step == 0)
    def _():
        a_all[...], r_all[...], ends[0], ends[1], ends[2], e_ref[...], _ = scan_factors(g_ref[...], d_ref[...])
        mask[...] = spread_mask()
        state[...] = jnp.zeros_like(state)

    row, col = iotas()
    lower = row >= col
    here = slab_at(step)
    scale = spread(a_all[here, :], mask[...])
    u2s = [(u_ref[chunk_rows(at), :].astype(F32) * scale[:, chunk_rows(at)]).astype(BF16) for at in range(PER)]
    b_ts = [b_ref[chunk_rows(at), :].T for at in range(PER)]
    cs = [c_ref[chunk_rows(at), :] for at in range(PER)]
    scores = [jnp.where(lower, mm(cs[at], b_ts[at]), 0.0).astype(BF16) for at in range(PER)]
    slabs = (ends[0, here, :], ends[1, here, :], ends[2, here, :])

    back = spread(r_all[here, :], mask[...])

    def finish(at, value):
        y_ref[chunk_rows(at), :] = (back[:, chunk_rows(at)] * value).astype(BF16)
        back_ref[chunk_rows(at), :] = back[:, chunk_rows(at)]

    local_scan(u2s, scores, b_ts, cs, slabs, state, finish)


def start_state(got_ref, state):
    me = lax.axis_index("seq")
    state[...] = jnp.zeros_like(state)
    for k in range(GROUPS - 1):

        @pl.when(k < me)
        def _():
            tail = got_ref[k, CHUNK:TAIL, :].astype(F32)
            decay = jnp.exp(tail[0:1] + tail[1:2] + tail[2:3])
            state[...] = decay * state[...] + got_ref[k, 0:CHUNK, :].astype(F32)


def add_start(y_ref, c_ref, back_ref, e_slab, state, out_ref, base=0):
    start = state[...]
    for at in range(PER):
        rows = chunk_rows(at)
        held = (start * row_pair(e_slab, at)).astype(BF16)
        value = y_ref[rows, :].astype(F32) + back_ref[rows, :] * mm(c_ref[rows, :], held)
        out_ref[pl.ds(pl.multiple_of(base + at * CHUNK, CHUNK), CHUNK), :] = value.astype(out_ref.dtype)


def read_lists(got_ref, slots):
    for k in range(GROUPS):
        lists = got_ref[k, TAIL:MSG, :].astype(F32)
        slots[4 * k : 4 * k + 4, :] = (lists[0:4] * 128.0 + lists[4:8]).astype(jnp.int32)


def take_rows(source, table, line, first, count):
    return jnp.concatenate([source[pl.ds(table[line, first + k], 1), :] for k in range(count)], axis=0)


def send_x_kernel(
    y_ref, c_ref, back_ref, e_ref, got_ref, out_ref, state, rows, slots, table, sem
):
    step = pl.program_id(0)

    @pl.when(step == 0)
    def _():
        read_lists(got_ref, slots)
        pltpu.make_async_copy(slots, table, sem).start()
        start_state(got_ref, state)

    @pl.when(step < STEPS)
    def _():
        base = step * STEP
        add_start(y_ref, c_ref, back_ref, e_ref[slab_at(step), :], state, rows, base)

    @pl.when(step == 0)
    def _():
        pltpu.make_async_copy(slots, table, sem).wait()

    @pl.when(step >= STEPS)
    def _():
        def take(i, _):
            for at in range(LINES):
                line = i * LINES + at
                for q in range(LANES // 16):
                    here = pl.ds(pl.multiple_of(line * LANES + q * 16, 16), 16)
                    out_ref[here, :] = take_rows(rows, table, (step - STEPS) * PER + line, q * 16, 16).astype(BF16)
            return 0

        lax.fori_loop(0, PER // LINES, take, 0)


def before_z_kernel(
    g_ref, d_ref, b_ref, c_ref, gate_ref,
    s_ref, b_t_ref, scale_ref, back_ref, t_ref, f_ref, e_ref, ends_ref, a_all, r_all, mask,
):
    step = pl.program_id(0)

    @pl.when(step == 0)
    def _():
        _, total = end_weights(g_ref[...], d_ref[...])
        t_ref[...] = jnp.broadcast_to(total, (8, LANES))
        a_all[...], r_all[...], ends_ref[0], ends_ref[1], ends_ref[2], e_ref[...], f_ref[...] = scan_factors(
            g_ref[...], d_ref[...]
        )
        mask[...] = spread_mask()

    row, col = iotas()
    lower = row >= col
    here = slab_at(step)
    scale = spread(a_all[here, :], mask[...])
    back = spread(r_all[here, :], mask[...])
    for at in range(PER):
        rows = chunk_rows(at)
        b_t = b_ref[rows, :].T
        b_t_ref[:, rows] = b_t
        s_ref[rows, :] = jnp.where(lower, mm(c_ref[rows, :], b_t), 0.0).astype(BF16)
        scale_ref[rows, :] = scale[:, rows]
        gate = gate_ref[rows, :].astype(F32)
        silu = gate * (0.5 * jnp.tanh(0.5 * gate) + 0.5)
        back_ref[rows, :] = silu * back[:, rows]


def states_z_kernel(
    place_ref, t_ref, f_ref, scale_ref, b_t_ref, got_ref, u2_ref, msg_ref, state, rows, place, sem
):
    step = pl.program_id(0)

    @pl.when(step == 0)
    def _():
        pltpu.make_async_copy(place_ref, place, sem).start()
        state[...] = jnp.zeros_like(state)

    @pl.when(step < STEPS)
    def _():
        rows[pl.ds(pl.multiple_of(step * STEP, STEP), STEP), :] = got_ref[...].astype(F32)

    @pl.when(step == 0)
    def _():
        pltpu.make_async_copy(place_ref, place, sem).wait()

    @pl.when(step >= STEPS)
    def _():
        block_at = step - STEPS

        def one(i, total):
            for at in range(TOGETHER):
                chunk = i * TOGETHER + at
                here = pl.ds(pl.multiple_of(chunk * CHUNK, CHUNK), CHUNK)
                line = block_at * PER + chunk
                u = take_rows(rows, place, line, 0, CHUNK)
                u2 = (u * scale_ref[here, :]).astype(BF16)
                u2_ref[here, :] = u2
                factor = by_head(f_ref[pl.ds(2 * line, 1), :], f_ref[pl.ds(2 * line + 1, 1), :])
                total = total + factor * mm(b_t_ref[:, here], u2)
            return total

        state[...] = lax.fori_loop(0, PER // TOGETHER, one, state[...])

    @pl.when(step == 2 * STEPS - 1)
    def _():
        write_tail(msg_ref, state[...], t_ref[0:1, :])


def local_z_kernel(u2_ref, s_ref, b_t_ref, c_ref, back_ref, ends_ref, y_ref, state):
    step = pl.program_id(0)

    @pl.when(step == 0)
    def _():
        state[...] = jnp.zeros_like(state)

    here = slab_at(step)
    u2s = [u2_ref[chunk_rows(at), :] for at in range(PER)]
    scores = [s_ref[chunk_rows(at), :] for at in range(PER)]
    b_ts = [b_t_ref[:, chunk_rows(at)] for at in range(PER)]
    cs = [c_ref[chunk_rows(at), :] for at in range(PER)]
    slabs = (ends_ref[0, here, :], ends_ref[1, here, :], ends_ref[2, here, :])

    def finish(at, value):
        y_ref[chunk_rows(at), :] = (back_ref[chunk_rows(at), :] * value).astype(BF16)

    local_scan(u2s, scores, b_ts, cs, slabs, state, finish)


def gate_z_kernel(y_ref, c_ref, back_ref, e_ref, got_ref, out_ref, state):
    step = pl.program_id(0)

    @pl.when(step == 0)
    def _():
        start_state(got_ref, state)

    add_start(y_ref, c_ref, back_ref, e_ref[slab_at(step), :], state, out_ref)


def final_kernel(x_ref, w_ref, out_ref):
    parts = [x_ref[k].astype(F32) for k in range(8)]
    squares = sum(part * part for part in parts)
    mean = jnp.sum(squares, axis=1, keepdims=True) * (1.0 / 1024.0)
    scale = lax.rsqrt(mean + 1e-05)
    normed = []
    for k in range(8):
        pieces_of = w_ref[k, LANES:WROWS, 0:LANES].astype(F32)
        gain = pieces_of[0:1] + pieces_of[1:2] + pieces_of[2:3]
        normed.append((parts[k] * scale * gain).astype(BF16))
    weight = jnp.concatenate([w_ref[k, 0:LANES, :] for k in range(8)], axis=0)
    out_ref[...] = mm(jnp.concatenate(normed, axis=1), weight).astype(BF16)


ROW = (STEP, LANES)
FLAT = (CHUNK, LANES)
GOT_X = (GROUPS, MSG, LANES)
GOT_Z = (GROUPS, TAIL, LANES)
ENDS = (3, CHUNK, LANES)
MASK = pltpu.VMEM((6 * PER, STEP), BF16)
STATE = pltpu.VMEM(FLAT, F32)


def block(shape, index):
    return pl.BlockSpec(shape, index)


def fixed(shape):
    return pl.BlockSpec(shape, lambda *_: (0,) * len(shape))


def each(i, *_):
    return (i, 0)


def early(i, *_):
    return (jnp.minimum(i, STEPS - 1), 0)


def late(i, *_):
    return (jnp.maximum(i - STEPS, 0), 0)


def struct(shape, dtype):
    return jax.ShapeDtypeStruct(shape, dtype)


def call(kernel, name, steps, ins, outs, shapes, scratch, mib, prefetch=0, limit=36, loose=-1):
    large = 1 << 13
    shapes = jax.tree.map(
        lambda shape: pltpu.HBM(shape.shape, shape.dtype) if math.prod(shape.shape) >= large else shape, shapes
    )
    made = pl.pallas_call(
        kernel,
        name=name,
        grid_spec=pltpu.PrefetchScalarGridSpec(
            num_scalar_prefetch=prefetch, grid=(steps,), in_specs=ins, out_specs=outs, scratch_shapes=scratch
        ),
        out_shape=shapes,
        compiler_params=pltpu.CompilerParams(
            dimension_semantics=("arbitrary",), vmem_limit_bytes=limit * 1024 * 1024
        ),
        cost_estimate=pl.CostEstimate(flops=mib << 28, bytes_accessed=mib << 20, transcendentals=0),
    )

    def run(*values):
        return made(
            *[
                pltpu.with_memory_space_constraint(value, pltpu.HBM)
                if at != loose and value.size >= large
                else value
                for at, value in enumerate(values)
            ]
        )

    return run


def states_x(z, g, d, b, u):
    return call(
        states_x_kernel, "states_x", STEPS,
        [fixed((64, LANES)), fixed(FLAT), fixed(FLAT), block(ROW, each), block(ROW, each)],
        [fixed(GOT_X), fixed((64, LANES))], [struct(GOT_X, BF16), struct((64, LANES), jnp.int32)],
        [STATE, MASK, STATE, pltpu.VMEM((8, LANES), F32)], 4,
    )(z, g, d, b, u)


def local_x(g, d, b, c, u):
    return call(
        local_x_kernel, "local_x", STEPS,
        [fixed(FLAT), fixed(FLAT), block(ROW, each), block(ROW, each), block(ROW, each)],
        [block(ROW, each), block(ROW, each), fixed(FLAT)],
        [struct((TOK, LANES), BF16), struct((TOK, LANES), F32), struct(FLAT, F32)],
        [STATE, STATE, pltpu.VMEM(ENDS, F32), MASK, STATE], 12,
    )(g, d, b, c, u)


def send_x(y, c, back, e, got):
    return call(
        send_x_kernel, "send_x", 2 * STEPS,
        [block(ROW, early), block(ROW, early), block(ROW, early), fixed(FLAT), fixed(GOT_X)],
        block(ROW, late), struct((TOK, LANES), BF16),
        [
            STATE, pltpu.VMEM((TOK, LANES), F32),
            pltpu.VMEM((64, LANES), jnp.int32), pltpu.SMEM((64, LANES), jnp.int32), pltpu.SemaphoreType.DMA,
        ], 12, loose=4,
    )(y, c, back, e, got)


def before_z(g, d, b, c, gate):
    return call(
        before_z_kernel, "before_z", STEPS,
        [fixed(FLAT), fixed(FLAT), block(ROW, each), block(ROW, each), block(ROW, each)],
        [
            block(ROW, each), block((CHUNK, STEP), lambda i: (0, i)), block(ROW, each), block(ROW, each),
            fixed((8, LANES)), fixed(FLAT), fixed(FLAT), fixed(ENDS),
        ],
        [
            struct((TOK, LANES), BF16), struct((CHUNK, TOK), BF16), struct((TOK, LANES), F32),
            struct((TOK, LANES), F32), struct((8, LANES), F32), struct(FLAT, F32), struct(FLAT, F32),
            struct(ENDS, F32),
        ],
        [STATE, STATE, MASK], 18,
    )(g, d, b, c, gate)


def states_z(place, t, f, scale, b_t, got):
    return call(
        states_z_kernel, "states_z", 2 * STEPS,
        [
            fixed((64, LANES)), fixed((8, LANES)), fixed(FLAT), block(ROW, late),
            block((CHUNK, STEP), lambda i: (0, jnp.maximum(i - STEPS, 0))), block(ROW, early),
        ],
        [block(ROW, late), fixed(GOT_Z)],
        [struct((TOK, LANES), BF16), struct(GOT_Z, BF16)],
        [
            STATE, pltpu.VMEM((TOK, LANES), F32), pltpu.SMEM((64, LANES), jnp.int32), pltpu.SemaphoreType.DMA,
        ], 10, loose=5,
    )(place, t, f, scale, b_t, got)


def local_z(u2, s, b_t, c, back, ends):
    return call(
        local_z_kernel, "local_z", STEPS,
        [
            block(ROW, each), block(ROW, each), block((CHUNK, STEP), lambda i: (0, i)), block(ROW, each),
            block(ROW, each), fixed(ENDS),
        ],
        block(ROW, each), struct((TOK, LANES), BF16), [STATE], 14,
    )(u2, s, b_t, c, back, ends)


def gate_z(y, c, back, e, got):
    return call(
        gate_z_kernel, "gate_z", STEPS,
        [block(ROW, each), block(ROW, each), block(ROW, each), fixed(FLAT), fixed(GOT_Z)],
        block(ROW, each), struct((TOK, LANES), BF16), [STATE], 12, loose=4,
    )(y, c, back, e, got)


def final(x, w):
    rows = 1024
    return call(
        final_kernel, "final", 1024 // rows,
        [block((8, rows, LANES), lambda i: (0, i, 0)), fixed((8, WROWS, 512))],
        block((rows, 512), each), struct((1024, 512), BF16), [], 5, limit=20, loose=0,
    )(x, w)


def three_pieces(value):
    high = lax.reduce_precision(value, 8, 7)
    mid = lax.reduce_precision(value - high, 8, 7)
    return high, mid, value - high - mid


def flat(value):
    return value.reshape(2, TOK // CHUNK, CHUNK).transpose(1, 0, 2).reshape(CHUNK, LANES)


def body(
    x_inputs,
    x_in_proj,
    x_out_proj,
    x_log_decay,
    x_step,
    z_source,
    z_in_proj,
    z_out_proj,
    z_log_decay,
    z_step,
    gate_branch,
    norm_gain,
    out_weight,
):
    g_x, d_x = flat(x_log_decay), flat(x_step)
    message, place = states_x(z_source.reshape(64, LANES), g_x, d_x, x_in_proj, x_inputs)
    message, g_x, d_x = lax.optimization_barrier((message, g_x, d_x))
    got_x = lax.all_to_all(message, "seq", 0, 0)
    y_x, back_x, e_x = local_x(g_x, d_x, x_in_proj, x_out_proj, x_inputs)
    sent = send_x(y_x, x_out_proj, back_x, e_x, got_x)
    sent, g_z, d_z, norm_gain, out_weight = lax.optimization_barrier(
        (sent, z_log_decay, z_step, norm_gain, out_weight)
    )
    gain = jnp.pad(jnp.stack(three_pieces(norm_gain)), ((0, WROWS - LANES - 3), (0, 512 - LANES))).astype(BF16)
    weights = lax.all_gather(jnp.concatenate([out_weight, gain], axis=0), "head", axis=0, tiled=False)
    received = lax.all_to_all(sent.reshape(GROUPS, PIECE, LANES), "seq", 0, 0).reshape(TOK, LANES)
    s_z, b_t, scale_z, back_z, t_z, f_z, e_z, ends_z = before_z(
        flat(g_z), flat(d_z), z_in_proj, z_out_proj, gate_branch
    )
    received, weights = lax.optimization_barrier((received, weights))
    u2_z, tails_z = states_z(place, t_z, f_z, scale_z, b_t, received)
    got_z = lax.all_to_all(tails_z, "seq", 0, 0)
    y_z = local_z(u2_z, s_z, b_t, z_out_proj, back_z, ends_z)
    gated = gate_z(y_z, z_out_proj, back_z, e_z, got_z)
    whole = lax.all_to_all(gated.reshape(8, 1024, LANES), "head", 0, 0)
    return final(whole, weights)


def solution(mesh):
    placed = (
        P("seq", "head"),
        P("seq", None),
        P("seq", None),
        P("head", "seq"),
        P("head", "seq"),
        P("seq"),
        P("seq", None),
        P("seq", None),
        P("head", "seq"),
        P("head", "seq"),
        P("seq", "head"),
        P("head"),
        P("head", None),
    )
    return jax.shard_map(
        body, mesh=mesh, in_specs=placed, out_specs=P(("seq", "head"), None), check_vma=False
    )
```
